128 devices in a mesh: pb: 4 (over z_hi, core), ka: 32 (over z_lo, y, x).
Axes of the slice: x: 4, y: 4, z: 4 (z_hi: 2, z_lo: 2; z = z_hi * 2 + z_lo), core: 2. Of those that a mesh axis runs over, the one named last changes fastest.
Arguments:
- vertex_ladder: float32 [2, 16, 1024, 1024], P(None, 'pb', 'ka'), may hold values from -6 to 6
- vertex_cross_a: float32 [2, 16, 1024, 1024], P(None, 'pb', 'ka'), may hold values from -6 to 6
- vertex_cross_b: float32 [2, 16, 1024, 1024], P(None, 'pb', 'ka'), may hold values from -6 to 6
- bubble: float32 [2, 16, 1024], P(None, 'pb'), may hold values from -0.072 to 0.072
- row_maps: int32 [2, 16, 1024], replicated, may hold values from 0 to 16383, as said below
- col_maps: int32 [2, 1024], replicated, may hold values from 0 to 1023, each once within a row
Outputs:
- ladder_out: float32 [2, 16, 1024, 1024], P(None, 'pb', 'ka')
- crossed_a: float32 [2, 16, 1024, 1024], P(None, 'pb', 'ka')
- crossed_b: float32 [2, 16, 1024, 1024], P(None, 'pb', 'ka')
The draws below stay inside these ranges and needn't reach their ends.
Inputs may be any that keep to these rules, and one draw needn't show every extreme that they name: `row_maps`: each of the two maps is a permutation of all 16384 rows. A device holds the rows of its bosonic indices (index of pb) and its first fermionic indices (index of ka); the 128 rows of one device take exactly 1 of their source rows from each device.
All inputs are finite; a program needn't handle non-finite values.
Results may differ from the reference program's by a relative error of at most 0.007.
Values may be sent and summed in bfloat16 or wider, within the bound.
A program may use at most 64 MiB of HBM per device.

```python
import jax
import jax.numpy as jnp
from jax import lax

K = 1024
Q_DEV = 4
LADDER = 6
Q = 16
ROWS = 32
DEVS = 128


def one_table(key):
    key_target, key_offset, key_source = jax.random.split(key, 3)
    count = Q_DEV * K // (K // ROWS)
    per_peer = count // DEVS
    ka_count = K // ROWS
    target_perm = jax.vmap(lambda sub: jax.random.permutation(sub, count))(jax.random.split(key_target, DEVS))
    offsets = jax.random.randint(key_offset, (DEVS,), 0, DEVS)
    source_perm = jax.vmap(lambda sub: jax.random.permutation(sub, count))(jax.random.split(key_source, DEVS))
    device_ids = jnp.arange(DEVS, dtype=jnp.int32)[:, None]
    source_dev = (target_perm % DEVS + offsets[:, None]) % DEVS
    source_slot = device_ids * per_peer + target_perm // DEVS
    source_local = source_perm[source_dev, source_slot]
    local_ids = jnp.arange(count, dtype=jnp.int32)[None, :]

    def global_row(device, local):
        bos = device // ka_count * Q_DEV + local // ROWS
        fer = device % ka_count * ROWS + local % ROWS
        return (bos * K + fer).astype(jnp.int32)
    target_rows = global_row(device_ids + 0 * local_ids, local_ids + 0 * device_ids).reshape(-1)
    source_rows = global_row(source_dev, source_local).reshape(-1)
    table = jnp.zeros((Q * K,), jnp.int32).at[target_rows].set(source_rows)
    return table.reshape(Q, K)


def draw_row_maps(key, part):
    return jnp.stack([one_table(jax.random.fold_in(key, 11)), one_table(jax.random.fold_in(key, 23))])


def level_of(key, extent, cuts, smallest, largest):
    def one(dim, blocks):
        steps = jax.random.uniform(jax.random.fold_in(jax.random.fold_in(key, 6), dim), (blocks,), jnp.float32, smallest / len(cuts), largest / len(cuts))
        return jnp.repeat(jnp.exp(steps), extent[dim] // blocks).reshape((-1,) + (1,) * (len(extent) - dim - 1))

    gain = one(*cuts[0])
    for cut in cuts[1:]:
        gain = gain * one(*cut)
    return gain


def noise(own_key, extent, width, most, pieces=(), kind=jnp.bfloat16):
    drawn = width * jax.random.normal(own_key, extent, jnp.float32)
    if pieces:
        drawn = drawn * level_of(own_key, extent, pieces, -0.22, 0.18)
    return jnp.clip(drawn, -most, most).astype(kind)


def setup_inputs(seed: int = 0) -> dict:
    splits = jax.random.split(jax.random.key(seed), 7)
    vertex_ladder = noise(splits[0], (2, Q, K, K), 1.0, 6.0, ((1, 4), (2, 32)), jnp.float32)
    vertex_cross_a = noise(splits[1], (2, Q, K, K), 1.0, 6.0, ((1, 4), (2, 32)), jnp.float32)
    vertex_cross_b = noise(splits[2], (2, Q, K, K), 1.0, 6.0, ((1, 4), (2, 32)), jnp.float32)
    bubble = noise(splits[3], (2, Q, K), 0.012, 0.072, ((1, 4),), jnp.float32)
    row_maps = draw_row_maps(jax.random.fold_in(splits[6], 71), 0)
    col_maps = jax.vmap(lambda own: jax.random.permutation(own, K))(jax.random.split(splits[5], 2)).reshape((2, K)).astype(jnp.int32)
    return {"vertex_ladder": vertex_ladder, "vertex_cross_a": vertex_cross_a, "vertex_cross_b": vertex_cross_b, "bubble": bubble, "row_maps": row_maps, "col_maps": col_maps}


def ladder_one(operands):
    vertex_q, bubble_q = operands
    lowered = vertex_q.astype(jnp.bfloat16)
    right_op = jnp.concatenate([lowered[0], lowered[1]], 1)
    row_count = vertex_q.shape[1]
    current = vertex_q
    for _ in range(LADDER):
        scaled_re = current[0] * bubble_q[0][None, :] - current[1] * bubble_q[1][None, :]
        scaled_im = current[0] * bubble_q[1][None, :] + current[1] * bubble_q[0][None, :]
        left_op = jnp.concatenate([scaled_re, scaled_im], 0).astype(jnp.bfloat16)
        product = jnp.dot(left_op, right_op, preferred_element_type=jnp.float32)
        real_part = product[:row_count, :K] - product[row_count:, K:]
        imag_part = product[:row_count, K:] + product[row_count:, :K]
        current = vertex_q + jnp.stack([real_part, imag_part])
    return current


def reference(vertex_ladder, vertex_cross_a, vertex_cross_b, bubble, row_maps, col_maps):
    full = lax.map(ladder_one, (jnp.moveaxis(vertex_ladder, 1, 0), jnp.moveaxis(bubble, 1, 0)))
    ladder_out = jnp.moveaxis(full, 0, 1)
    reducible = (ladder_out - vertex_ladder).reshape(2, Q * K, K)

    def cross(channel, base):
        picked = jnp.take(reducible, row_maps[channel].reshape(-1).astype(jnp.int32), axis=1)
        picked = jnp.take(picked, col_maps[channel].astype(jnp.int32), axis=2)
        return base + picked.reshape(2, Q, K, K)

    return ladder_out, cross(0, vertex_cross_a), cross(1, vertex_cross_b)
```

```python
import jax
import jax.numpy as jnp
from jax import lax
from jax.experimental import pallas as pl
from jax.experimental.pallas import tpu as pltpu
from jax.sharding import PartitionSpec as P

LADDER = 6
MESH = pl.DeviceIdType.MESH
BF16 = jnp.bfloat16
F32 = jnp.float32
K = 1024
ROWS = 32
QL = 4
MINE = 4 * ROWS
NB = 256


def ladder_kernel(
    vertex_ref, bubble_ref, home_ref, low, whole, base, full, left_op, outgoing,
    chi, send1, send_chi, recv_chi, recv, send2, send3, send_home, recv_home,
):
    pb, ka = lax.axis_index("pb"), lax.axis_index("ka")
    z_hi, core = pb // 2, pb % 2
    z_lo, y, x = ka // 16, (ka // 4) % 4, ka % 4
    line = ka - x

    def taker(j):
        return (z_hi * 2 + 1 - z_lo, core * 16 + j * 4 + x)

    def giver(j):
        return (z_hi * 2 + z_lo, (1 - core) * 16 + j * 4 + x)

    right = (pb, line + (x + 1) % 4)
    left = (pb, line + (x + 3) % 4)
    partner = (z_hi * 2 + 1 - core, ka)

    barrier = pltpu.get_barrier_semaphore()
    for j in range(4):
        pl.semaphore_signal(barrier, inc=1, device_id=taker(j), device_id_type=MESH)
        pl.semaphore_signal(barrier, inc=1, device_id=giver(j), device_id_type=MESH)
    for other in (right, left, partner):
        pl.semaphore_signal(barrier, inc=1, device_id=other, device_id_type=MESH)
    for j in range(4):
        low[j] = vertex_ref[:, j].astype(BF16)
    pl.semaphore_wait(barrier, 11)

    def rows_of(piece):
        return pl.ds(pl.multiple_of(piece * ROWS, ROWS), ROWS)

    def copy1(j):
        return pltpu.make_async_remote_copy(
            src_ref=low.at[j],
            dst_ref=whole.at[:, rows_of(ka), :],
            send_sem=send1.at[j],
            recv_sem=recv.at[ka],
            device_id=taker(j),
            device_id_type=MESH,
        )

    def pass_on(piece, sem, target):
        block = whole.at[:, rows_of(piece), :]
        return pltpu.make_async_remote_copy(
            src_ref=block,
            dst_ref=block,
            send_sem=sem,
            recv_sem=recv.at[piece],
            device_id=target,
            device_id_type=MESH,
        )

    def piece_at(j, shift):
        return (1 - core) * 16 + j * 4 + (x + shift) % 4

    def chi_copy(j, slot):
        return pltpu.make_async_remote_copy(
            src_ref=bubble_ref.at[j],
            dst_ref=chi.at[slot],
            send_sem=send_chi.at[j],
            recv_sem=recv_chi.at[slot],
            device_id=taker(j),
            device_id_type=MESH,
        )

    for j in range(4):
        copy1(j).start()
        chi_copy(j, y).start()
    for j in range(4):
        piece = piece_at(j, 0)
        pass_on(piece, send2.at[j, 0], right).wait_recv()
        pass_on(piece, send2.at[j, 0], right).start()
        pass_on(piece, send2.at[j, 1], left).start()
        pass_on(piece, send3.at[j, 0], partner).start()
    for j in range(4):
        piece = piece_at(j, 3)
        pass_on(piece, send3.at[j, 1], partner).wait_recv()
        if j < 2:
            pass_on(piece, send2.at[j, 2], right).start()
        pass_on(piece, send3.at[j, 1], partner).start()
        piece = piece_at(j, 1)
        pass_on(piece, send3.at[j, 2], partner).wait_recv()
        if j >= 2:
            pass_on(piece, send2.at[j, 2], left).start()
        pass_on(piece, send3.at[j, 2], partner).start()
    for j in range(4):
        piece = piece_at(j, 2)
        pass_on(piece, send3.at[j, 3], partner).wait_recv()
        pass_on(piece, send3.at[j, 3], partner).start()

    for j in range(4):
        rows = whole[:, rows_of(piece_at(j, 0)), :].astype(F32)
        base[:, j * ROWS:(j + 1) * ROWS, :] = rows
        full[:, j * ROWS:(j + 1) * ROWS, :] = rows
    for i in range(16):
        pass_on(core * 16 + i, send3.at[0, 0], partner).wait_recv()

    for j in range(4):
        chi_copy(j, j).wait_recv()
    chi_re = chi[0, 0:1, :]
    chi_im = chi[0, 1:2, :]

    def scale(i, carry):
        rows = pl.ds(pl.multiple_of(i * ROWS, ROWS), ROWS)
        re, im = full[0, rows, :], full[1, rows, :]
        left_op[rows, :] = (re * chi_re - im * chi_im).astype(BF16)
        low_rows = pl.ds(pl.multiple_of(MINE + i * ROWS, ROWS), ROWS)
        left_op[low_rows, :] = (re * chi_im + im * chi_re).astype(BF16)
        return carry

    def product(cols):
        by_re = jnp.dot(left_op[...], whole[0, :, cols], preferred_element_type=F32)
        by_im = jnp.dot(left_op[...], whole[1, :, cols], preferred_element_type=F32)
        return by_re[:MINE] - by_im[MINE:], by_im[:MINE] + by_re[MINE:]

    def step(_, carry):
        lax.fori_loop(0, MINE // ROWS, scale, 0)

        def columns(n, inner):
            cols = pl.ds(pl.multiple_of(n * NB, NB), NB)
            re, im = product(cols)
            full[0, :, cols] = base[0, :, cols] + re
            full[1, :, cols] = base[1, :, cols] + im
            return inner

        return lax.fori_loop(0, K // NB, columns, carry)

    lax.fori_loop(0, LADDER - 1, step, 0)
    lax.fori_loop(0, MINE // ROWS, scale, 0)

    def last(n, carry):
        cols = pl.ds(pl.multiple_of(n * NB, NB), NB)
        re, im = product(cols)
        for j in range(4):
            outgoing[j, 0, :, cols] = re[j * ROWS:(j + 1) * ROWS].astype(BF16)
            outgoing[j, 1, :, cols] = im[j * ROWS:(j + 1) * ROWS].astype(BF16)
        return carry

    lax.fori_loop(0, K // NB, last, 0)

    def home_copy(j):
        return pltpu.make_async_remote_copy(
            src_ref=outgoing.at[j],
            dst_ref=home_ref.at[y],
            send_sem=send_home.at[j],
            recv_sem=recv_home.at[y],
            device_id=giver(j),
            device_id_type=MESH,
        )

    def from_home(j):
        return pltpu.make_async_remote_copy(
            src_ref=outgoing.at[j],
            dst_ref=home_ref.at[j],
            send_sem=send_home.at[j],
            recv_sem=recv_home.at[j],
            device_id=taker(j),
            device_id_type=MESH,
        )

    for j in range(4):
        home_copy(j).start()
    for j in range(4):
        copy1(j).wait_send()
        chi_copy(j, j).wait_send()
        for t in range(3):
            pass_on(piece_at(j, 0), send2.at[j, t], right).wait_send()
        for t in range(4):
            pass_on(piece_at(j, 0), send3.at[j, t], partner).wait_send()
    for j in range(4):
        from_home(j).wait_recv()
        home_copy(j).wait_send()


def run_ladder(vertex, bubble):
    vmem = pl.BlockSpec(memory_space=pltpu.VMEM)
    return pl.pallas_call(
        ladder_kernel,
        out_shape=jax.ShapeDtypeStruct((QL, 2, ROWS, K), BF16),
        in_specs=[vmem, vmem],
        out_specs=vmem,
        scratch_shapes=[
            pltpu.VMEM((QL, 2, ROWS, K), BF16),
            pltpu.VMEM((2, K, K), BF16),
            pltpu.VMEM((2, MINE, K), F32),
            pltpu.VMEM((2, MINE, K), F32),
            pltpu.VMEM((2 * MINE, K), BF16),
            pltpu.VMEM((QL, 2, ROWS, K), BF16),
            pltpu.VMEM((4, 2, K), F32),
            pltpu.SemaphoreType.DMA((4,)),
            pltpu.SemaphoreType.DMA((4,)),
            pltpu.SemaphoreType.DMA((4,)),
            pltpu.SemaphoreType.DMA((32,)),
            pltpu.SemaphoreType.DMA((4, 3)),
            pltpu.SemaphoreType.DMA((4, 4)),
            pltpu.SemaphoreType.DMA((4,)),
            pltpu.SemaphoreType.DMA((4,)),
        ],
        compiler_params=pltpu.CompilerParams(
            collective_id=0, has_side_effects=True, vmem_limit_bytes=40 * 2**20
        ),
    )(vertex, bubble)


def per_device(vertex_ladder, vertex_cross_a, vertex_cross_b, bubble, row_maps, col_maps):
    q_local = vertex_ladder.shape[1]
    row_count = vertex_ladder.shape[2]
    col_count = vertex_ladder.shape[3]
    pb_count = lax.axis_size("pb")
    ka_count = lax.axis_size("ka")
    dev_count = pb_count * ka_count
    local_count = q_local * row_count
    pb, ka = lax.axis_index("pb"), lax.axis_index("ka")
    home = run_ladder(vertex_ladder, jnp.moveaxis(bubble, 1, 0))
    home = jnp.moveaxis(home, 1, 0)
    ladder_out = vertex_ladder + home.astype(F32)
    reducible = home.reshape(2, local_count, col_count)
    my_device = pb * ka_count + ka
    my_bos = pb * q_local + jnp.arange(q_local, dtype=jnp.int32)
    my_fer = ka * row_count + jnp.arange(row_count, dtype=jnp.int32)

    def device_of(global_rows):
        return global_rows // col_count // q_local * ka_count + global_rows % col_count // row_count

    def prepare(table):
        by_device = (
            table.reshape(pb_count, q_local, ka_count, row_count)
            .transpose(0, 2, 1, 3)
            .reshape(dev_count, local_count)
        )
        mine = (device_of(by_device) == my_device).astype(jnp.int32)
        source_local = (
            by_device // col_count % q_local * row_count + by_device % col_count % row_count
        )
        send_index = jnp.sum(mine * source_local, 1)
        return jnp.take(reducible, send_index, axis=1)

    def place(table, received, column_map):
        source = lax.dynamic_slice(table, (pb * q_local, ka * row_count), (q_local, row_count))
        picked = jnp.take(received, device_of(source.reshape(-1)), axis=1)
        selector = (jnp.arange(col_count, dtype=jnp.int32)[:, None] == column_map[None, :]).astype(BF16)
        picked = jnp.einsum("prk,km->prm", picked, selector, preferred_element_type=F32)
        return picked.reshape(2, q_local, row_count, col_count)

    both = jnp.concatenate([prepare(row_maps[0]), prepare(row_maps[1])], axis=0)
    both = lax.all_to_all(both, ("pb", "ka"), split_axis=1, concat_axis=1, tiled=True)
    crossed_a = vertex_cross_a + place(row_maps[0], both[:2], col_maps[0])
    crossed_b = vertex_cross_b + place(row_maps[1], both[2:], col_maps[1])
    return (ladder_out, crossed_a, crossed_b)


def solution(mesh):
    return jax.shard_map(
        per_device,
        mesh=mesh,
        in_specs=(
            P(None, "pb", "ka", None),
            P(None, "pb", "ka", None),
            P(None, "pb", "ka", None),
            P(None, "pb", None),
            P(),
            P(),
        ),
        out_specs=(P(None, "pb", "ka", None), P(None, "pb", "ka", None), P(None, "pb", "ka", None)),
        check_vma=False,
    )
```

```python
import jax
import jax.numpy as jnp
from jax import lax
from jax.experimental import pallas as pl
from jax.experimental.pallas import tpu as pltpu
from jax.sharding import PartitionSpec as P

LADDER = 6
MESH = pl.DeviceIdType.MESH
BF16 = jnp.bfloat16
F32 = jnp.float32
I32 = jnp.int32
K = 1024
ROWS = 32
QL = 4
MINE = 4 * ROWS
NB = 256
DEVS = 128
LANES = 128
TILE = 2 * K // LANES


def ladder_kernel(
    order_ref, vertex_ref, bubble_ref, col_ref, home_ref, crossed_ref,
    low, whole, base, full, left_op, outgoing, chi_own, chi, selector, sorted_rows, stage, packed,
    send1, send_chi, recv_chi, recv, send2, send3, send_home, recv_home,
    send_row, recv_row, own_row, known_half, known_all,
):
    pb, ka = lax.axis_index("pb"), lax.axis_index("ka")
    z_hi, core = pb // 2, pb % 2
    z_lo, y, x = ka // 16, (ka // 4) % 4, ka % 4
    line = ka - x
    me = pb * 32 + ka

    def taker(j):
        return (z_hi * 2 + 1 - z_lo, core * 16 + j * 4 + x)

    def giver(j):
        return (z_hi * 2 + z_lo, (1 - core) * 16 + j * 4 + x)

    right = (pb, line + (x + 1) % 4)
    left = (pb, line + (x + 3) % 4)
    partner = (z_hi * 2 + 1 - core, ka)
    across = (pb, (ka + 16) % 32)
    mirror = ((pb + 2) % 4, ka)

    barrier = pltpu.get_barrier_semaphore()
    for j in range(4):
        pl.semaphore_signal(barrier, inc=1, device_id=taker(j), device_id_type=MESH)
        pl.semaphore_signal(barrier, inc=1, device_id=giver(j), device_id_type=MESH)
    for other in (right, left, partner, across, mirror):
        pl.semaphore_signal(barrier, inc=1, device_id=other, device_id_type=MESH)
    for j in range(4):
        low[j] = vertex_ref[:, j].astype(BF16)
        chi_own[j] = bubble_ref[:, j]
    pl.semaphore_wait(barrier, 13)

    def rows_of(piece):
        return pl.ds(pl.multiple_of(piece * ROWS, ROWS), ROWS)

    def copy1(s):
        j = (y + s) % 4
        return pltpu.make_async_remote_copy(
            src_ref=low.at[j],
            dst_ref=whole.at[:, rows_of(ka), :],
            send_sem=send1.at[s],
            recv_sem=recv.at[ka],
            device_id=taker(j),
            device_id_type=MESH,
        )

    def chi_copy(s, slot):
        j = (y + s) % 4
        return pltpu.make_async_remote_copy(
            src_ref=chi_own.at[j],
            dst_ref=chi.at[slot],
            send_sem=send_chi.at[s],
            recv_sem=recv_chi.at[slot],
            device_id=taker(j),
            device_id_type=MESH,
        )

    def pass_on(piece, sem, target):
        block = whole.at[:, rows_of(piece), :]
        return pltpu.make_async_remote_copy(
            src_ref=block,
            dst_ref=block,
            send_sem=sem,
            recv_sem=recv.at[piece],
            device_id=target,
            device_id_type=MESH,
        )

    def piece_at(s, shift):
        return (1 - core) * 16 + (y + 4 - s) % 4 * 4 + (x + shift) % 4

    for s in range(4):
        copy1(s).start()
    for s in range(4):
        chi_copy(s, y).start()

    def select_rows(i, carry):
        at = pl.multiple_of(i * ROWS, ROWS)
        source = lax.broadcasted_iota(I32, (ROWS, K), 0) + at
        for c in range(2):
            hit = source == col_ref[c:c + 1, :]
            selector[c, pl.ds(at, ROWS), :] = jnp.where(hit, 1.0, 0.0).astype(BF16)
        return carry

    lax.fori_loop(0, K // ROWS, select_rows, 0)

    for s in range(4):
        piece = piece_at(s, 0)
        pass_on(piece, send2.at[s, 0], right).wait_recv()
        pass_on(piece, send2.at[s, 0], right).start()
        pass_on(piece, send2.at[s, 1], left).start()
        pass_on(piece, send3.at[s, 0], partner).start()
    for s in range(4):
        piece = piece_at(s, 3)
        pass_on(piece, send3.at[s, 1], partner).wait_recv()
        if s < 2:
            pass_on(piece, send2.at[s, 2], right).start()
        pass_on(piece, send3.at[s, 1], partner).start()
        piece = piece_at(s, 1)
        pass_on(piece, send3.at[s, 2], partner).wait_recv()
        if s >= 2:
            pass_on(piece, send2.at[s, 2], left).start()
        pass_on(piece, send3.at[s, 2], partner).start()
    for s in range(4):
        piece = piece_at(s, 2)
        pass_on(piece, send3.at[s, 3], partner).wait_recv()
        pass_on(piece, send3.at[s, 3], partner).start()

    for j in range(4):
        rows = whole[:, rows_of((1 - core) * 16 + j * 4 + x), :].astype(F32)
        base[:, j * ROWS:(j + 1) * ROWS, :] = rows
        full[:, j * ROWS:(j + 1) * ROWS, :] = rows
    for i in range(16):
        pass_on(core * 16 + i, send3.at[0, 0], partner).wait_recv()
    pl.semaphore_signal(known_half, inc=1, device_id=across, device_id_type=MESH)

    for s in range(4):
        chi_copy(s, s).wait_recv()
    chi_re = chi[0, 0:1, :]
    chi_im = chi[0, 1:2, :]

    def scale(i, carry):
        rows = pl.ds(pl.multiple_of(i * ROWS, ROWS), ROWS)
        re, im = full[0, rows, :], full[1, rows, :]
        left_op[rows, :] = (re * chi_re - im * chi_im).astype(BF16)
        low_rows = pl.ds(pl.multiple_of(MINE + i * ROWS, ROWS), ROWS)
        left_op[low_rows, :] = (re * chi_im + im * chi_re).astype(BF16)
        return carry

    def product(cols):
        by_re = jnp.dot(left_op[...], whole[0, :, cols], preferred_element_type=F32)
        by_im = jnp.dot(left_op[...], whole[1, :, cols], preferred_element_type=F32)
        return by_re[:MINE] - by_im[MINE:], by_im[:MINE] + by_re[MINE:]

    def step(_, carry):
        lax.fori_loop(0, MINE // ROWS, scale, 0)

        def columns(n, inner):
            cols = pl.ds(pl.multiple_of(n * NB, NB), NB)
            re, im = product(cols)
            full[0, :, cols] = base[0, :, cols] + re
            full[1, :, cols] = base[1, :, cols] + im
            return inner

        return lax.fori_loop(0, K // NB, columns, carry)

    lax.fori_loop(0, 2, step, 0)
    pl.semaphore_wait(known_half, 1)
    pl.semaphore_signal(known_all, inc=1, device_id=mirror, device_id_type=MESH)
    lax.fori_loop(0, LADDER - 3, step, 0)
    lax.fori_loop(0, MINE // ROWS, scale, 0)

    def last(n, carry):
        cols = pl.ds(pl.multiple_of(n * NB, NB), NB)
        re, im = product(cols)
        for j in range(4):
            outgoing[j, 0, :, cols] = re[j * ROWS:(j + 1) * ROWS].astype(BF16)
            outgoing[j, 1, :, cols] = im[j * ROWS:(j + 1) * ROWS].astype(BF16)
        return carry

    lax.fori_loop(0, K // NB, last, 0)

    def home_copy(s):
        j = (y + s) % 4
        return pltpu.make_async_remote_copy(
            src_ref=outgoing.at[j],
            dst_ref=home_ref.at[y],
            send_sem=send_home.at[s],
            recv_sem=recv_home.at[y],
            device_id=giver(j),
            device_id_type=MESH,
        )

    def from_home(j):
        return pltpu.make_async_remote_copy(
            src_ref=outgoing.at[j],
            dst_ref=home_ref.at[j],
            send_sem=send_home.at[j],
            recv_sem=recv_home.at[j],
            device_id=taker(j),
            device_id_type=MESH,
        )

    for s in range(4):
        home_copy(s).start()
    for s in range(4):
        copy1(s).wait_send()
        chi_copy(s, s).wait_send()
        for t in range(3):
            pass_on(piece_at(s, 0), send2.at[s, t], right).wait_send()
        for t in range(4):
            pass_on(piece_at(s, 0), send3.at[s, t], partner).wait_send()
    for j in range(4):
        from_home(j).wait_recv()
    pl.semaphore_wait(known_all, 1)

    def row_copy(c, target, slot):
        return pltpu.make_async_remote_copy(
            src_ref=packed.at[c, target],
            dst_ref=crossed_ref.at[c, slot],
            send_sem=send_row.at[c],
            recv_sem=recv_row.at[c],
            device_id=(target // 32, target % 32),
            device_id_type=MESH,
        )

    def own_copy(c):
        return pltpu.make_async_copy(packed.at[c, me], crossed_ref.at[c, me], own_row.at[c])

    for c in range(2):
        for p in range(2):
            rows = home_ref[:, p].reshape(MINE, K)
            sorted_rows[p * DEVS:(p + 1) * DEVS, :] = jnp.dot(
                order_ref[c], rows, preferred_element_type=F32
            ).astype(BF16)

        def cross_columns(n, carry):
            cols = pl.ds(pl.multiple_of(n * NB, NB), NB)
            moved = jnp.dot(sorted_rows[...], selector[c, :, cols], preferred_element_type=F32)
            for p in range(2):
                for h in range(NB // LANES):
                    start = p * (TILE // 2) + n * (NB // LANES) + h
                    stage[pl.ds(start, DEVS, stride=TILE), :] = moved[
                        p * DEVS:(p + 1) * DEVS, h * LANES:(h + 1) * LANES
                    ]
            return carry

        lax.fori_loop(0, K // NB, cross_columns, 0)

        def pack(t, carry):
            packed[c, t] = stage[pl.ds(pl.multiple_of(t * TILE, TILE), TILE), :].astype(BF16)
            return carry

        lax.fori_loop(0, DEVS, pack, 0, unroll=8)

        def send(i, carry):
            row_copy(c, (me + i) % DEVS, me).start()
            return carry

        lax.fori_loop(1, DEVS, send, 0)
        own_copy(c).start()

    for c in range(2):
        others = pltpu.make_async_remote_copy(
            src_ref=packed.at[c, pl.ds(0, DEVS - 1)],
            dst_ref=crossed_ref.at[c, pl.ds(0, DEVS - 1)],
            send_sem=send_row.at[c],
            recv_sem=recv_row.at[c],
            device_id=right,
            device_id_type=MESH,
        )
        others.wait_recv()
        others.wait_send()
        own_copy(c).wait()
    for s in range(4):
        home_copy(s).wait_send()


def run_ladder(order, vertex, bubble, col_maps):
    vmem = pl.BlockSpec(memory_space=pltpu.VMEM)
    return pl.pallas_call(
        ladder_kernel,
        out_shape=(
            jax.ShapeDtypeStruct((QL, 2, ROWS, K), BF16),
            jax.ShapeDtypeStruct((2, DEVS, TILE, LANES), BF16),
        ),
        in_specs=[vmem, vmem, vmem, vmem],
        out_specs=(vmem, pl.BlockSpec(memory_space=pl.ANY)),
        scratch_shapes=[
            pltpu.VMEM((QL, 2, ROWS, K), BF16),
            pltpu.VMEM((2, K, K), BF16),
            pltpu.VMEM((2, MINE, K), F32),
            pltpu.VMEM((2, MINE, K), F32),
            pltpu.VMEM((2 * MINE, K), BF16),
            pltpu.VMEM((QL, 2, ROWS, K), BF16),
            pltpu.VMEM((QL, 2, K), F32),
            pltpu.VMEM((QL, 2, K), F32),
            pltpu.VMEM((2, K, K), BF16),
            pltpu.VMEM((2 * DEVS, K), BF16),
            pltpu.VMEM((DEVS * TILE, LANES), F32),
            pltpu.VMEM((2, DEVS, TILE, LANES), BF16),
            pltpu.SemaphoreType.DMA((4,)),
            pltpu.SemaphoreType.DMA((4,)),
            pltpu.SemaphoreType.DMA((4,)),
            pltpu.SemaphoreType.DMA((32,)),
            pltpu.SemaphoreType.DMA((4, 3)),
            pltpu.SemaphoreType.DMA((4, 4)),
            pltpu.SemaphoreType.DMA((4,)),
            pltpu.SemaphoreType.DMA((4,)),
            pltpu.SemaphoreType.DMA((2,)),
            pltpu.SemaphoreType.DMA((2,)),
            pltpu.SemaphoreType.DMA((2,)),
            pltpu.SemaphoreType.REGULAR,
            pltpu.SemaphoreType.REGULAR,
        ],
        compiler_params=pltpu.CompilerParams(
            collective_id=0, has_side_effects=True, vmem_limit_bytes=44 * 2**20
        ),
    )(order, vertex, bubble, col_maps)


def finish_kernel(source_ref, home_ref, crossed_ref, vertex_ref, a_ref, b_ref, out_ref, out_a_ref, out_b_ref, stage):
    q = pl.program_id(0)
    for p in range(2):
        out_ref[p, 0] = vertex_ref[p, 0] + home_ref[0, p].astype(F32)
    for c, (add_ref, to_ref) in enumerate(((a_ref, out_a_ref), (b_ref, out_b_ref))):

        def place(r, carry):
            at = pl.multiple_of(r * TILE, TILE)
            stage[c, pl.ds(at, TILE), :] = crossed_ref[c, source_ref[c, q * ROWS + r]].astype(F32)
            return carry

        lax.fori_loop(0, ROWS, place, 0, unroll=8)
        for p in range(2):
            for h in range(K // LANES):
                cols = slice(h * LANES, (h + 1) * LANES)
                moved = stage[c, pl.ds(p * (TILE // 2) + h, ROWS, stride=TILE), :]
                to_ref[p, 0, :, cols] = add_ref[p, 0, :, cols] + moved


def finish(source, home, crossed, vertex, cross_a, cross_b):
    whole_block = pl.BlockSpec((2, DEVS, TILE, LANES), lambda q: (0, 0, 0, 0), pipeline_mode=pl.Buffered(1))
    row_block = pl.BlockSpec((2, 1, ROWS, K), lambda q: (0, q, 0, 0))
    shape = jax.ShapeDtypeStruct(vertex.shape, F32)
    return pl.pallas_call(
        finish_kernel,
        grid=(QL,),
        out_shape=(shape, shape, shape),
        in_specs=[
            pl.BlockSpec(memory_space=pltpu.SMEM),
            pl.BlockSpec((1, 2, ROWS, K), lambda q: (q, 0, 0, 0)),
            whole_block,
            row_block,
            row_block,
            row_block,
        ],
        out_specs=(row_block, row_block, row_block),
        scratch_shapes=[pltpu.VMEM((2, ROWS * TILE, LANES), F32)],
    )(source, home, crossed, vertex, cross_a, cross_b)


def per_device(vertex_ladder, vertex_cross_a, vertex_cross_b, bubble, row_maps, col_maps):
    q_local = vertex_ladder.shape[1]
    row_count = vertex_ladder.shape[2]
    col_count = vertex_ladder.shape[3]
    pb_count = lax.axis_size("pb")
    ka_count = lax.axis_size("ka")
    dev_count = pb_count * ka_count
    local_count = q_local * row_count
    pb, ka = lax.axis_index("pb"), lax.axis_index("ka")
    my_device = pb * ka_count + ka

    def device_of(rows):
        return rows // col_count // q_local * ka_count + rows % col_count // row_count

    by_device = (
        row_maps.reshape(2, pb_count, q_local, ka_count, row_count)
        .transpose(0, 1, 3, 2, 4)
        .reshape(2, dev_count, local_count)
    )
    local = by_device // col_count % q_local * row_count + by_device % row_count
    send_index = jnp.sum(jnp.where(device_of(by_device) == my_device, local, 0), 2)
    order = (send_index[:, :, None] == jnp.arange(local_count, dtype=I32)).astype(BF16)
    mine = lax.dynamic_slice(row_maps, (0, pb * q_local, ka * row_count), (2, q_local, row_count))
    source = device_of(mine).reshape(2, local_count)
    home, crossed = run_ladder(order, vertex_ladder, bubble, col_maps)
    return finish(source, home, crossed, vertex_ladder, vertex_cross_a, vertex_cross_b)


def solution(mesh):
    return jax.shard_map(
        per_device,
        mesh=mesh,
        in_specs=(
            P(None, "pb", "ka", None),
            P(None, "pb", "ka", None),
            P(None, "pb", "ka", None),
            P(None, "pb", None),
            P(),
            P(),
        ),
        out_specs=(P(None, "pb", "ka", None), P(None, "pb", "ka", None), P(None, "pb", "ka", None)),
        check_vma=False,
    )
```

```python
import jax
import jax.numpy as jnp
from jax import lax
from jax.experimental import pallas as pl
from jax.experimental.pallas import tpu as pltpu
from jax.sharding import PartitionSpec as P

LADDER = 6
MESH = pl.DeviceIdType.MESH
BF16 = jnp.bfloat16
F32 = jnp.float32
I32 = jnp.int32
K = 1024
ROWS = 32
QL = 4
MINE = QL * ROWS
NB = 256
DEVS = 128
LANES = 128
HALF = K // 2
TILE = 16
BLOCKS = HALF // LANES
OVER_ROWS = (((0,), (0,)), ((), ()))


def one_hot(hit):
    return jnp.where(hit, 1.0, 0.0).astype(BF16)


def ladder_kernel(
    vertex_ref, bubble_ref, row_ref, col_ref, home_ref, to_a_ref, to_b_ref,
    vertex, low, whole, base, left_op, outgoing, home, chi_own, chi, selector, send_order, place_order,
    stage, packed, arrived, lined_up, placed,
    load, send1, send_chi, recv_chi, recv, send2, send3, send_home, recv_home,
    send_row, recv_row, own_row, known_half, known_all,
):
    pb, ka = lax.axis_index("pb"), lax.axis_index("ka")
    z_hi, core = pb // 2, pb % 2
    z_lo, y, x = ka // 16, (ka // 4) % 4, ka % 4
    line = ka - x
    me = pb * 32 + ka

    def taker(j):
        return (z_hi * 2 + 1 - z_lo, core * 16 + j * 4 + x)

    def giver(j):
        return (z_hi * 2 + z_lo, (1 - core) * 16 + j * 4 + x)

    right = (pb, line + (x + 1) % 4)
    left = (pb, line + (x + 3) % 4)
    partner = (z_hi * 2 + 1 - core, ka)
    across = (pb, (ka + 16) % 32)
    mirror = ((pb + 2) % 4, ka)

    vertex_copy = pltpu.make_async_copy(vertex_ref, vertex, load)
    vertex_copy.start()
    barrier = pltpu.get_barrier_semaphore()
    for j in range(4):
        pl.semaphore_signal(barrier, inc=1, device_id=taker(j), device_id_type=MESH)
        pl.semaphore_signal(barrier, inc=1, device_id=giver(j), device_id_type=MESH)
    for other in (right, left, partner, across, mirror):
        pl.semaphore_signal(barrier, inc=1, device_id=other, device_id_type=MESH)
    for j in range(QL):
        chi_own[j] = bubble_ref[:, j]
    vertex_copy.wait()
    for j in range(QL):
        low[j] = vertex[:, j].astype(BF16)
    pl.semaphore_wait(barrier, 13)

    def rows_of(piece):
        return pl.ds(pl.multiple_of(piece * ROWS, ROWS), ROWS)

    def copy1(s):
        j = (y + s) % 4
        return pltpu.make_async_remote_copy(
            src_ref=low.at[j],
            dst_ref=whole.at[:, rows_of(ka), :],
            send_sem=send1.at[s],
            recv_sem=recv.at[ka],
            device_id=taker(j),
            device_id_type=MESH,
        )

    def chi_copy(s, slot):
        j = (y + s) % 4
        return pltpu.make_async_remote_copy(
            src_ref=chi_own.at[j],
            dst_ref=chi.at[slot],
            send_sem=send_chi.at[s],
            recv_sem=recv_chi.at[slot],
            device_id=taker(j),
            device_id_type=MESH,
        )

    def pass_on(piece, sem, target):
        block = whole.at[:, rows_of(piece), :]
        return pltpu.make_async_remote_copy(
            src_ref=block,
            dst_ref=block,
            send_sem=sem,
            recv_sem=recv.at[piece],
            device_id=target,
            device_id_type=MESH,
        )

    def pass_plane(piece, plane, sem, target):
        block = whole.at[plane, rows_of(piece), :]
        return pltpu.make_async_remote_copy(
            src_ref=block,
            dst_ref=block,
            send_sem=sem,
            recv_sem=recv.at[piece],
            device_id=target,
            device_id_type=MESH,
        )

    def piece_at(s, shift):
        return (1 - core) * 16 + (y + 4 - s) % 4 * 4 + (x + shift) % 4

    for s in range(4):
        copy1(s).start()
    for s in range(4):
        chi_copy(s, y).start()

    for s in range(4):
        piece = piece_at(s, 0)
        pass_on(piece, send2.at[s, 0], right).wait_recv()
        pass_on(piece, send2.at[s, 0], right).start()
        pass_on(piece, send2.at[s, 1], left).start()
        pass_on(piece, send3.at[s, 0], partner).start()

    def select_rows(i, carry):
        at = pl.multiple_of(i * ROWS, ROWS)
        source = lax.broadcasted_iota(I32, (ROWS, K), 0) + at
        for c in range(2):
            selector[c, pl.ds(at, ROWS), :] = one_hot(source == col_ref[c:c + 1, :])
        return carry

    lax.fori_loop(0, K // ROWS, select_rows, 0)
    at_row = lax.broadcasted_iota(I32, (K, LANES), 0)
    at_lane = lax.broadcasted_iota(I32, (K, LANES), 1)
    by_ka = one_hot((at_lane % 32) == (at_row // 32))
    by_own = one_hot(((at_lane % 32) == (at_row % 32)) & ((at_row // 32) == ka))
    table_row = lax.broadcasted_iota(I32, (16, LANES), 0)
    table_lane = lax.broadcasted_iota(I32, (16, LANES), 1)
    for c in range(2):
        table = row_ref[c]
        owner = table // (QL * K) * 32 + table % K // ROWS
        local = table // K % QL * ROWS + table % ROWS
        wanted = jnp.where(owner == me, local + 1, 0).astype(F32).astype(BF16)
        wanted = jnp.dot(wanted, by_ka, preferred_element_type=F32)
        wanted = jnp.where(table_row // QL == table_lane // 32, wanted, 0.0)
        wanted = jnp.sum(wanted, axis=0, keepdims=True)
        local_row = (lax.broadcasted_iota(I32, (MINE, DEVS), 0) + 1).astype(F32)
        send_order[:, c * DEVS:(c + 1) * DEVS] = one_hot(local_row == wanted)
        owner = jnp.dot(owner.astype(F32).astype(BF16), by_own, preferred_element_type=F32)
        owner = jnp.where(table_row == pb * QL + table_lane // 32, owner, 0.0)
        owner = jnp.sum(owner, axis=0, keepdims=True)
        device = lax.broadcasted_iota(I32, (DEVS, MINE), 0).astype(F32)
        place_order[c] = one_hot(device == owner)

    for s in range(4):
        piece = piece_at(s, 3)
        pass_on(piece, send3.at[s, 1], partner).wait_recv()
        pass_plane(piece, 0, send2.at[s, 2], right).start()
        pass_on(piece, send3.at[s, 1], partner).start()
        piece = piece_at(s, 1)
        pass_on(piece, send3.at[s, 2], partner).wait_recv()
        pass_plane(piece, 1, send2.at[s, 3], left).start()
        pass_on(piece, send3.at[s, 2], partner).start()

    for s in range(4):
        chi_copy(s, s).wait_recv()

    def scaled(re, im, cols):
        chi_re, chi_im = chi[0, 0:1, cols], chi[0, 1:2, cols]
        return (re * chi_re - im * chi_im).astype(BF16), (re * chi_im + im * chi_re).astype(BF16)

    for j in range(4):
        at = j * ROWS
        rows = whole[:, rows_of((1 - core) * 16 + j * 4 + x), :].astype(F32)
        base[:, at:at + ROWS, :] = rows
        left_op[0, at:at + ROWS, :], left_op[0, MINE + at:MINE + at + ROWS, :] = scaled(rows[0], rows[1], slice(0, K))

    for s in range(4):
        piece = piece_at(s, 2)
        pass_on(piece, send3.at[s, 3], partner).wait_recv()
        pass_on(piece, send3.at[s, 3], partner).start()
    for i in range(16):
        pass_on(core * 16 + i, send3.at[0, 0], partner).wait_recv()
    pl.semaphore_signal(known_half, inc=1, device_id=across, device_id_type=MESH)

    def product(now, n):
        cols = slice(n * NB, (n + 1) * NB)
        by_re = jnp.dot(left_op[now], whole[0, :, cols], preferred_element_type=F32)
        by_im = jnp.dot(left_op[now], whole[1, :, cols], preferred_element_type=F32)
        return by_re[:MINE] - by_im[MINE:], by_im[:MINE] + by_re[MINE:]

    def step(i, carry):
        now = i % 2
        for n in range(K // NB):
            cols = slice(n * NB, (n + 1) * NB)
            re, im = product(now, n)
            re, im = scaled(base[0, :, cols] + re, base[1, :, cols] + im, cols)
            left_op[1 - now, 0:MINE, cols] = re
            left_op[1 - now, MINE:2 * MINE, cols] = im
        return carry

    lax.fori_loop(0, 2, step, 0)
    pl.semaphore_wait(known_half, 1)
    pl.semaphore_signal(known_all, inc=1, device_id=mirror, device_id_type=MESH)
    lax.fori_loop(2, LADDER - 1, step, 0)

    def home_copy(h, s):
        j = (y + s) % 4
        return pltpu.make_async_remote_copy(
            src_ref=outgoing.at[h, j],
            dst_ref=home.at[h, y],
            send_sem=send_home.at[h, s],
            recv_sem=recv_home.at[h, y],
            device_id=giver(j),
            device_id_type=MESH,
        )

    def from_home(h, j):
        return pltpu.make_async_remote_copy(
            src_ref=outgoing.at[h, j],
            dst_ref=home.at[h, j],
            send_sem=send_home.at[h, j],
            recv_sem=recv_home.at[h, j],
            device_id=taker(j),
            device_id_type=MESH,
        )

    for n in range(K // NB):
        re, im = product((LADDER - 1) % 2, n)
        h = n * NB // HALF
        cols = slice(n * NB % HALF, n * NB % HALF + NB)
        for j in range(4):
            outgoing[h, j, 0, :, cols] = re[j * ROWS:(j + 1) * ROWS].astype(BF16)
            outgoing[h, j, 1, :, cols] = im[j * ROWS:(j + 1) * ROWS].astype(BF16)
        if (n + 1) * NB % HALF == 0:
            for s in range(4):
                home_copy(h, s).start()

    for s in range(4):
        copy1(s).wait_send()
        chi_copy(s, s).wait_send()
        for t in range(2):
            pass_on(piece_at(s, 0), send2.at[s, t], right).wait_send()
        for t in range(2, 4):
            pass_plane(piece_at(s, 0), 0, send2.at[s, t], right).wait_send()
        for t in range(4):
            pass_on(piece_at(s, 0), send3.at[s, t], partner).wait_send()

    def row_copy(h, target):
        return pltpu.make_async_remote_copy(
            src_ref=packed.at[h, target],
            dst_ref=arrived.at[h, me],
            send_sem=send_row.at[h],
            recv_sem=recv_row.at[h],
            device_id=(target // 32, target % 32),
            device_id_type=MESH,
        )

    def own_copy(h):
        return pltpu.make_async_copy(packed.at[h, me], arrived.at[h, me], own_row.at[h])

    def others(h):
        return pltpu.make_async_remote_copy(
            src_ref=packed.at[h, pl.ds(0, DEVS - 1)],
            dst_ref=arrived.at[h, pl.ds(0, DEVS - 1)],
            send_sem=send_row.at[h],
            recv_sem=recv_row.at[h],
            device_id=right,
            device_id_type=MESH,
        )

    for h in range(2):
        for s in range(4):
            from_home(h, s).wait_recv()
        if h == 0:
            pl.semaphore_wait(known_all, 1)
        for p in range(2):
            rows = home[h, :, p].reshape(MINE, HALF)
            ordered = lax.dot_general(send_order[...], rows, OVER_ROWS, preferred_element_type=F32)
            for c in range(2):
                for b in range(BLOCKS):
                    stage[pl.ds((c * 2 + p) * BLOCKS + b, DEVS, stride=TILE), :] = ordered[
                        c * DEVS:(c + 1) * DEVS, b * LANES:(b + 1) * LANES
                    ]

        def pack(t, carry):
            packed[h, t] = stage[pl.ds(pl.multiple_of(t * TILE, TILE), TILE), :].astype(BF16)
            return carry

        lax.fori_loop(0, DEVS, pack, 0, unroll=8)

        def send(i, carry):
            row_copy(h, (me + i) % DEVS).start()
            return carry

        lax.fori_loop(1, DEVS, send, 0)
        own_copy(h).start()

    for h in range(2):
        for p in range(2):
            for q in range(QL):
                home_ref[p, q, :, h * HALF:(h + 1) * HALF] = home[h, q, p]

    for h in range(2):
        others(h).wait_recv()
        own_copy(h).wait()

        def unpack(t, carry):
            stage[pl.ds(pl.multiple_of(t * TILE, TILE), TILE), :] = arrived[h, t].astype(F32)
            return carry

        lax.fori_loop(0, DEVS, unpack, 0, unroll=8)
        for b in range(4 * BLOCKS):
            lined_up[:, b * LANES:(b + 1) * LANES] = stage[pl.ds(b, DEVS, stride=TILE), :].astype(BF16)
        for c, to_ref in enumerate((to_a_ref, to_b_ref)):
            for p in range(2):
                rows = lined_up[:, (c * 2 + p) * HALF:(c * 2 + p + 1) * HALF]
                placed[p * MINE:(p + 1) * MINE, :] = lax.dot_general(
                    place_order[c], rows, OVER_ROWS, preferred_element_type=F32
                ).astype(BF16)
            for n in range(K // NB):
                cols = slice(n * NB, (n + 1) * NB)
                moved = jnp.dot(
                    placed[...], selector[c, h * HALF:(h + 1) * HALF, cols], preferred_element_type=F32
                )
                moved = moved.reshape(2, QL, ROWS, NB)
                if h == 0:
                    to_ref[:, :, :, cols] = moved.astype(BF16)
                else:
                    to_ref[:, :, :, cols] = (to_ref[:, :, :, cols].astype(F32) + moved).astype(BF16)

    for h in range(2):
        others(h).wait_send()
        for s in range(4):
            home_copy(h, s).wait_send()


def run_ladder(vertex, bubble, row_maps, col_maps):
    vmem = pl.BlockSpec(memory_space=pltpu.VMEM)
    out = jax.ShapeDtypeStruct((2, QL, ROWS, K), BF16)
    return pl.pallas_call(
        ladder_kernel,
        out_shape=(out, out, out),
        in_specs=[pl.BlockSpec(memory_space=pl.ANY), vmem, vmem, vmem],
        out_specs=(vmem, vmem, vmem),
        scratch_shapes=[
            pltpu.VMEM((2, QL, ROWS, K), F32),
            pltpu.VMEM((QL, 2, ROWS, K), BF16),
            pltpu.VMEM((2, K, K), BF16),
            pltpu.VMEM((2, MINE, K), F32),
            pltpu.VMEM((2, 2 * MINE, K), BF16),
            pltpu.VMEM((2, QL, 2, ROWS, HALF), BF16),
            pltpu.VMEM((2, QL, 2, ROWS, HALF), BF16),
            pltpu.VMEM((QL, 2, K), F32),
            pltpu.VMEM((QL, 2, K), F32),
            pltpu.VMEM((2, K, K), BF16),
            pltpu.VMEM((MINE, 2 * DEVS), BF16),
            pltpu.VMEM((2, DEVS, MINE), BF16),
            pltpu.VMEM((DEVS * TILE, LANES), F32),
            pltpu.VMEM((2, DEVS, TILE, LANES), BF16),
            pltpu.VMEM((2, DEVS, TILE, LANES), BF16),
            pltpu.VMEM((DEVS, 4 * HALF), BF16),
            pltpu.VMEM((2 * MINE, HALF), BF16),
            pltpu.SemaphoreType.DMA,
            pltpu.SemaphoreType.DMA((4,)),
            pltpu.SemaphoreType.DMA((4,)),
            pltpu.SemaphoreType.DMA((4,)),
            pltpu.SemaphoreType.DMA((32,)),
            pltpu.SemaphoreType.DMA((4, 4)),
            pltpu.SemaphoreType.DMA((4, 4)),
            pltpu.SemaphoreType.DMA((2, 4)),
            pltpu.SemaphoreType.DMA((2, 4)),
            pltpu.SemaphoreType.DMA((2,)),
            pltpu.SemaphoreType.DMA((2,)),
            pltpu.SemaphoreType.DMA((2,)),
            pltpu.SemaphoreType.REGULAR,
            pltpu.SemaphoreType.REGULAR,
        ],
        compiler_params=pltpu.CompilerParams(
            collective_id=0, has_side_effects=True, vmem_limit_bytes=56 * 2**20
        ),
    )(vertex, bubble, row_maps, col_maps)


def per_device(vertex_ladder, vertex_cross_a, vertex_cross_b, bubble, row_maps, col_maps):
    home, to_a, to_b = run_ladder(vertex_ladder, bubble, row_maps, col_maps)
    return (
        vertex_ladder + home.astype(F32),
        vertex_cross_a + to_a.astype(F32),
        vertex_cross_b + to_b.astype(F32),
    )


def solution(mesh):
    return jax.shard_map(
        per_device,
        mesh=mesh,
        in_specs=(
            P(None, "pb", "ka", None),
            P(None, "pb", "ka", None),
            P(None, "pb", "ka", None),
            P(None, "pb", None),
            P(),
            P(),
        ),
        out_specs=(P(None, "pb", "ka", None), P(None, "pb", "ka", None), P(None, "pb", "ka", None)),
        check_vma=False,
    )
```

```python
import jax
import jax.numpy as jnp
from jax import lax
from jax.experimental import pallas as pl
from jax.experimental.pallas import tpu as pltpu
from jax.sharding import PartitionSpec as P

LADDER = 6
MESH = pl.DeviceIdType.MESH
BF16 = jnp.bfloat16
F32 = jnp.float32
I32 = jnp.int32
K = 1024
ROWS = 32
QL = 4
MINE = QL * ROWS
NB = 256
DEVS = 128
LANES = 128
HALF = K // 2
TILE = 16
BLOCKS = HALF // LANES
OVER_ROWS = (((0,), (0,)), ((), ()))


def one_hot(hit):
    return jnp.where(hit, 1.0, 0.0).astype(BF16)


def ladder_kernel(
    vertex_ref, bubble_ref, row_ref, col_ref, home_ref, to_a_ref, to_b_ref,
    vertex, low, whole, base, left_even, left_odd, outgoing, home, chi_own, chi, selector, send_order, place_order,
    stage, packed, arrived, lined_up, placed,
    load, send1, send_chi, recv_chi, recv, send2, send3, send_home, recv_home,
    send_row, recv_row, own_row, known_half, known_all,
):
    pb, ka = lax.axis_index("pb"), lax.axis_index("ka")
    z_hi, core = pb // 2, pb % 2
    z_lo, y, x = ka // 16, (ka // 4) % 4, ka % 4
    line = ka - x
    me = pb * 32 + ka

    def taker(j):
        return (z_hi * 2 + 1 - z_lo, core * 16 + j * 4 + x)

    def giver(j):
        return (z_hi * 2 + z_lo, (1 - core) * 16 + j * 4 + x)

    right = (pb, line + (x + 1) % 4)
    left = (pb, line + (x + 3) % 4)
    partner = (z_hi * 2 + 1 - core, ka)
    across = (pb, (ka + 16) % 32)
    mirror = ((pb + 2) % 4, ka)

    vertex_copy = pltpu.make_async_copy(vertex_ref, vertex, load)
    vertex_copy.start()
    barrier = pltpu.get_barrier_semaphore()
    for j in range(4):
        pl.semaphore_signal(barrier, inc=1, device_id=taker(j), device_id_type=MESH)
        pl.semaphore_signal(barrier, inc=1, device_id=giver(j), device_id_type=MESH)
    for other in (right, left, partner, across, mirror):
        pl.semaphore_signal(barrier, inc=1, device_id=other, device_id_type=MESH)
    for j in range(QL):
        chi_own[j] = bubble_ref[:, j]
    vertex_copy.wait()
    for j in range(QL):
        low[j] = vertex[:, j].astype(BF16)
    pl.semaphore_wait(barrier, 13)

    def rows_of(piece):
        return pl.ds(pl.multiple_of(piece * ROWS, ROWS), ROWS)

    def copy1(s):
        j = (y + s) % 4
        return pltpu.make_async_remote_copy(
            src_ref=low.at[j],
            dst_ref=whole.at[:, rows_of(ka), :],
            send_sem=send1.at[s],
            recv_sem=recv.at[ka],
            device_id=taker(j),
            device_id_type=MESH,
        )

    def chi_copy(s, slot):
        j = (y + s) % 4
        return pltpu.make_async_remote_copy(
            src_ref=chi_own.at[j],
            dst_ref=chi.at[slot],
            send_sem=send_chi.at[s],
            recv_sem=recv_chi.at[slot],
            device_id=taker(j),
            device_id_type=MESH,
        )

    def pass_on(piece, sem, target):
        block = whole.at[:, rows_of(piece), :]
        return pltpu.make_async_remote_copy(
            src_ref=block,
            dst_ref=block,
            send_sem=sem,
            recv_sem=recv.at[piece],
            device_id=target,
            device_id_type=MESH,
        )

    def pass_plane(piece, plane, sem, target):
        block = whole.at[plane, rows_of(piece), :]
        return pltpu.make_async_remote_copy(
            src_ref=block,
            dst_ref=block,
            send_sem=sem,
            recv_sem=recv.at[piece],
            device_id=target,
            device_id_type=MESH,
        )

    def piece_at(s, shift):
        return (1 - core) * 16 + (y + 4 - s) % 4 * 4 + (x + shift) % 4

    for s in range(4):
        copy1(s).start()
    for s in range(4):
        chi_copy(s, y).start()

    for s in range(4):
        piece = piece_at(s, 0)
        pass_on(piece, send2.at[s, 0], right).wait_recv()
        pass_on(piece, send2.at[s, 0], right).start()
        pass_on(piece, send2.at[s, 1], left).start()
        pass_on(piece, send3.at[s, 0], partner).start()

    def select_rows(i, carry):
        at = pl.multiple_of(i * ROWS, ROWS)
        source = lax.broadcasted_iota(I32, (ROWS, K), 0) + at
        for c in range(2):
            selector[c, pl.ds(at, ROWS), :] = one_hot(source == col_ref[c:c + 1, :])
        return carry

    lax.fori_loop(0, K // ROWS, select_rows, 0)
    at_row = lax.broadcasted_iota(I32, (K, LANES), 0)
    at_lane = lax.broadcasted_iota(I32, (K, LANES), 1)
    by_ka = one_hot((at_lane % 32) == (at_row // 32))
    by_own = one_hot(((at_lane % 32) == (at_row % 32)) & ((at_row // 32) == ka))
    table_row = lax.broadcasted_iota(I32, (16, LANES), 0)
    table_lane = lax.broadcasted_iota(I32, (16, LANES), 1)
    for c in range(2):
        table = row_ref[c]
        owner = table // (QL * K) * 32 + table % K // ROWS
        local = table // K % QL * ROWS + table % ROWS
        wanted = jnp.where(owner == me, local + 1, 0).astype(F32).astype(BF16)
        wanted = jnp.dot(wanted, by_ka, preferred_element_type=F32)
        wanted = jnp.where(table_row // QL == table_lane // 32, wanted, 0.0)
        wanted = jnp.sum(wanted, axis=0, keepdims=True)
        local_row = (lax.broadcasted_iota(I32, (MINE, DEVS), 0) + 1).astype(F32)
        send_order[:, c * DEVS:(c + 1) * DEVS] = one_hot(local_row == wanted)
        owner = jnp.dot(owner.astype(F32).astype(BF16), by_own, preferred_element_type=F32)
        owner = jnp.where(table_row == pb * QL + table_lane // 32, owner, 0.0)
        owner = jnp.sum(owner, axis=0, keepdims=True)
        device = lax.broadcasted_iota(I32, (DEVS, MINE), 0).astype(F32)
        place_order[c] = one_hot(device == owner)

    for s in range(4):
        piece = piece_at(s, 3)
        pass_on(piece, send3.at[s, 1], partner).wait_recv()
        pass_plane(piece, 0, send2.at[s, 2], right).start()
        pass_on(piece, send3.at[s, 1], partner).start()
        piece = piece_at(s, 1)
        pass_on(piece, send3.at[s, 2], partner).wait_recv()
        pass_plane(piece, 1, send2.at[s, 3], left).start()
        pass_on(piece, send3.at[s, 2], partner).start()

    for s in range(4):
        chi_copy(s, s).wait_recv()

    def scaled(re, im, cols):
        chi_re, chi_im = chi[0, 0:1, cols], chi[0, 1:2, cols]
        return (re * chi_re - im * chi_im).astype(BF16), (re * chi_im + im * chi_re).astype(BF16)

    for j in range(4):
        at = j * ROWS
        rows = whole[:, rows_of((1 - core) * 16 + j * 4 + x), :]
        base[:, at:at + ROWS, :] = rows
        re, im = scaled(rows[0].astype(F32), rows[1].astype(F32), slice(0, K))
        left_even[at:at + ROWS, :] = re
        left_even[MINE + at:MINE + at + ROWS, :] = im

    for s in range(4):
        piece = piece_at(s, 2)
        pass_on(piece, send3.at[s, 3], partner).wait_recv()
        pass_on(piece, send3.at[s, 3], partner).start()
    for i in range(16):
        pass_on(core * 16 + i, send3.at[0, 0], partner).wait_recv()
    pl.semaphore_signal(known_half, inc=1, device_id=across, device_id_type=MESH)

    def product(left_op, n):
        cols = slice(n * NB, (n + 1) * NB)
        by_re = jnp.dot(left_op[...], whole[0, :, cols], preferred_element_type=F32)
        by_im = jnp.dot(left_op[...], whole[1, :, cols], preferred_element_type=F32)
        return by_re[:MINE] - by_im[MINE:], by_im[:MINE] + by_re[MINE:]

    def step(now, later):
        for n in range(K // NB):
            cols = slice(n * NB, (n + 1) * NB)
            re, im = product(now, n)
            re, im = scaled(base[0, :, cols].astype(F32) + re, base[1, :, cols].astype(F32) + im, cols)
            later[0:MINE, cols] = re
            later[MINE:2 * MINE, cols] = im

    def two_steps(i, carry):
        step(left_even, left_odd)
        step(left_odd, left_even)

        @pl.when(i == 0)
        def _():
            pl.semaphore_wait(known_half, 1)
            pl.semaphore_signal(known_all, inc=1, device_id=mirror, device_id_type=MESH)

        return carry

    lax.fori_loop(0, LADDER // 2 - 1, two_steps, 0)
    step(left_even, left_odd)

    def home_copy(h, s):
        j = (y + s) % 4
        return pltpu.make_async_remote_copy(
            src_ref=outgoing.at[h, j],
            dst_ref=home.at[h, y],
            send_sem=send_home.at[h, s],
            recv_sem=recv_home.at[h, y],
            device_id=giver(j),
            device_id_type=MESH,
        )

    def from_home(h, j):
        return pltpu.make_async_remote_copy(
            src_ref=outgoing.at[h, j],
            dst_ref=home.at[h, j],
            send_sem=send_home.at[h, j],
            recv_sem=recv_home.at[h, j],
            device_id=taker(j),
            device_id_type=MESH,
        )

    for n in range(K // NB):
        re, im = product(left_odd, n)
        h = n * NB // HALF
        cols = slice(n * NB % HALF, n * NB % HALF + NB)
        for j in range(4):
            outgoing[h, j, 0, :, cols] = re[j * ROWS:(j + 1) * ROWS].astype(BF16)
            outgoing[h, j, 1, :, cols] = im[j * ROWS:(j + 1) * ROWS].astype(BF16)
        if (n + 1) * NB % HALF == 0:
            for s in range(4):
                home_copy(h, s).start()

    for s in range(4):
        copy1(s).wait_send()
        chi_copy(s, s).wait_send()
        for t in range(2):
            pass_on(piece_at(s, 0), send2.at[s, t], right).wait_send()
        for t in range(2, 4):
            pass_plane(piece_at(s, 0), 0, send2.at[s, t], right).wait_send()
        for t in range(4):
            pass_on(piece_at(s, 0), send3.at[s, t], partner).wait_send()

    def row_copy(h, target):
        return pltpu.make_async_remote_copy(
            src_ref=packed.at[h, target],
            dst_ref=arrived.at[h, me],
            send_sem=send_row.at[h],
            recv_sem=recv_row.at[h],
            device_id=(target // 32, target % 32),
            device_id_type=MESH,
        )

    def own_copy(h):
        return pltpu.make_async_copy(packed.at[h, me], arrived.at[h, me], own_row.at[h])

    def others(h):
        return pltpu.make_async_remote_copy(
            src_ref=packed.at[h, pl.ds(0, DEVS - 1)],
            dst_ref=arrived.at[h, pl.ds(0, DEVS - 1)],
            send_sem=send_row.at[h],
            recv_sem=recv_row.at[h],
            device_id=right,
            device_id_type=MESH,
        )

    for h in range(2):
        for s in range(4):
            from_home(h, s).wait_recv()
        if h == 0:
            pl.semaphore_wait(known_all, 1)
        for p in range(2):
            rows = home[h, :, p].reshape(MINE, HALF)
            ordered = lax.dot_general(send_order[...], rows, OVER_ROWS, preferred_element_type=F32)
            for c in range(2):
                for b in range(BLOCKS):
                    stage[pl.ds((c * 2 + p) * BLOCKS + b, DEVS, stride=TILE), :] = ordered[
                        c * DEVS:(c + 1) * DEVS, b * LANES:(b + 1) * LANES
                    ]

        def pack(t, carry):
            packed[h, t] = stage[pl.ds(pl.multiple_of(t * TILE, TILE), TILE), :].astype(BF16)
            return carry

        lax.fori_loop(0, DEVS, pack, 0, unroll=8)

        def send(i, carry):
            row_copy(h, (me + i) % DEVS).start()
            return carry

        lax.fori_loop(1, DEVS, send, 0)
        own_copy(h).start()

    for h in range(2):
        for p in range(2):
            for q in range(QL):
                home_ref[p, q, :, h * HALF:(h + 1) * HALF] = home[h, q, p]

    for h in range(2):
        others(h).wait_recv()
        own_copy(h).wait()

        def unpack(t, carry):
            stage[pl.ds(pl.multiple_of(t * TILE, TILE), TILE), :] = arrived[h, t].astype(F32)
            return carry

        lax.fori_loop(0, DEVS, unpack, 0, unroll=8)
        for b in range(4 * BLOCKS):
            lined_up[:, b * LANES:(b + 1) * LANES] = stage[pl.ds(b, DEVS, stride=TILE), :].astype(BF16)
        for c, to_ref in enumerate((to_a_ref, to_b_ref)):
            for p in range(2):
                rows = lined_up[:, (c * 2 + p) * HALF:(c * 2 + p + 1) * HALF]
                placed[p * MINE:(p + 1) * MINE, :] = lax.dot_general(
                    place_order[c], rows, OVER_ROWS, preferred_element_type=F32
                ).astype(BF16)
            for n in range(K // NB):
                cols = slice(n * NB, (n + 1) * NB)
                moved = jnp.dot(
                    placed[...], selector[c, h * HALF:(h + 1) * HALF, cols], preferred_element_type=F32
                )
                moved = moved.reshape(2, QL, ROWS, NB)
                if h == 0:
                    to_ref[:, :, :, cols] = moved.astype(BF16)
                else:
                    to_ref[:, :, :, cols] = (to_ref[:, :, :, cols].astype(F32) + moved).astype(BF16)

    for h in range(2):
        others(h).wait_send()
        for s in range(4):
            home_copy(h, s).wait_send()


def run_ladder(vertex, bubble, row_maps, col_maps):
    vmem = pl.BlockSpec(memory_space=pltpu.VMEM)
    out = jax.ShapeDtypeStruct((2, QL, ROWS, K), BF16)
    return pl.pallas_call(
        ladder_kernel,
        out_shape=(out, out, out),
        in_specs=[pl.BlockSpec(memory_space=pl.ANY), vmem, vmem, vmem],
        out_specs=(vmem, vmem, vmem),
        scratch_shapes=[
            pltpu.VMEM((2, QL, ROWS, K), F32),
            pltpu.VMEM((QL, 2, ROWS, K), BF16),
            pltpu.VMEM((2, K, K), BF16),
            pltpu.VMEM((2, MINE, K), BF16),
            pltpu.VMEM((2 * MINE, K), BF16),
            pltpu.VMEM((2 * MINE, K), BF16),
            pltpu.VMEM((2, QL, 2, ROWS, HALF), BF16),
            pltpu.VMEM((2, QL, 2, ROWS, HALF), BF16),
            pltpu.VMEM((QL, 2, K), F32),
            pltpu.VMEM((QL, 2, K), F32),
            pltpu.VMEM((2, K, K), BF16),
            pltpu.VMEM((MINE, 2 * DEVS), BF16),
            pltpu.VMEM((2, DEVS, MINE), BF16),
            pltpu.VMEM((DEVS * TILE, LANES), F32),
            pltpu.VMEM((2, DEVS, TILE, LANES), BF16),
            pltpu.VMEM((2, DEVS, TILE, LANES), BF16),
            pltpu.VMEM((DEVS, 4 * HALF), BF16),
            pltpu.VMEM((2 * MINE, HALF), BF16),
            pltpu.SemaphoreType.DMA,
            pltpu.SemaphoreType.DMA((4,)),
            pltpu.SemaphoreType.DMA((4,)),
            pltpu.SemaphoreType.DMA((4,)),
            pltpu.SemaphoreType.DMA((32,)),
            pltpu.SemaphoreType.DMA((4, 4)),
            pltpu.SemaphoreType.DMA((4, 4)),
            pltpu.SemaphoreType.DMA((2, 4)),
            pltpu.SemaphoreType.DMA((2, 4)),
            pltpu.SemaphoreType.DMA((2,)),
            pltpu.SemaphoreType.DMA((2,)),
            pltpu.SemaphoreType.DMA((2,)),
            pltpu.SemaphoreType.REGULAR,
            pltpu.SemaphoreType.REGULAR,
        ],
        compiler_params=pltpu.CompilerParams(
            collective_id=0, has_side_effects=True, vmem_limit_bytes=28 * 2**20
        ),
    )(vertex, bubble, row_maps, col_maps)


def per_device(vertex_ladder, vertex_cross_a, vertex_cross_b, bubble, row_maps, col_maps):
    home, to_a, to_b = run_ladder(vertex_ladder, bubble, row_maps, col_maps)
    return (
        vertex_ladder + home.astype(F32),
        vertex_cross_a + to_a.astype(F32),
        vertex_cross_b + to_b.astype(F32),
    )


def solution(mesh):
    return jax.shard_map(
        per_device,
        mesh=mesh,
        in_specs=(
            P(None, "pb", "ka", None),
            P(None, "pb", "ka", None),
            P(None, "pb", "ka", None),
            P(None, "pb", None),
            P(),
            P(),
        ),
        out_specs=(P(None, "pb", "ka", None), P(None, "pb", "ka", None), P(None, "pb", "ka", None)),
        check_vma=False,
    )
```

```python
import jax
import jax.numpy as jnp
from jax import lax
from jax.experimental import pallas as pl
from jax.experimental.pallas import tpu as pltpu
from jax.sharding import PartitionSpec as P

LADDER = 6
MESH = pl.DeviceIdType.MESH
BF16 = jnp.bfloat16
F32 = jnp.float32
I32 = jnp.int32
K = 1024
ROWS = 32
QL = 4
MINE = QL * ROWS
NB = 256
DEVS = 128
LANES = 128
HALF = K // 2
TILE = 16
BLOCKS = HALF // LANES
OVER_ROWS = (((0,), (0,)), ((), ()))


def one_hot(hit):
    return jnp.where(hit, 1.0, 0.0).astype(BF16)


def ladder_kernel(
    vertex_ref, a_ref, b_ref, bubble_ref, row_ref, col_ref, to_ref, to_a_ref, to_b_ref,
    out_ref, out_a_ref, out_b_ref, bubble, rows_from, cols_from, low, whole, base, left_even, left_odd, outgoing, home, chi_own, chi, selector, send_order, place_order,
    stage, packed, arrived, lined_up, placed,
    load, store, send1, send_chi, recv_chi, recv, send2, send3, send_home, recv_home,
    send_row, recv_row, own_row, known_half, known_all,
):
    pb, ka = lax.axis_index("pb"), lax.axis_index("ka")
    z_hi, core = pb // 2, pb % 2
    z_lo, y, x = ka // 16, (ka // 4) % 4, ka % 4
    line = ka - x
    me = pb * 32 + ka

    def taker(j):
        return (z_hi * 2 + 1 - z_lo, core * 16 + j * 4 + x)

    def giver(j):
        return (z_hi * 2 + z_lo, (1 - core) * 16 + j * 4 + x)

    right = (pb, line + (x + 1) % 4)
    left = (pb, line + (x + 3) % 4)
    partner = (z_hi * 2 + 1 - core, ka)
    across = (pb, (ka + 16) % 32)
    mirror = ((pb + 2) % 4, ka)

    loads = [
        pltpu.make_async_copy(source, target, load.at[i])
        for i, (source, target) in enumerate((
            (vertex_ref, out_ref), (bubble_ref, bubble), (row_ref, rows_from), (col_ref, cols_from),
            (a_ref, out_a_ref), (b_ref, out_b_ref),
        ))
    ]
    loads[0].start()
    loads[1].start()
    barrier = pltpu.get_barrier_semaphore()
    for j in range(4):
        pl.semaphore_signal(barrier, inc=1, device_id=taker(j), device_id_type=MESH)
        pl.semaphore_signal(barrier, inc=1, device_id=giver(j), device_id_type=MESH)
    for other in (right, left, partner, across, mirror):
        pl.semaphore_signal(barrier, inc=1, device_id=other, device_id_type=MESH)
    loads[1].wait()
    for j in range(QL):
        chi_own[j] = bubble[:, j]
    loads[0].wait()
    for j in range(QL):
        low[j] = out_ref[:, j].astype(BF16)
    pl.semaphore_wait(barrier, 13)

    def rows_of(piece):
        return pl.ds(pl.multiple_of(piece * ROWS, ROWS), ROWS)

    def copy1(s):
        j = (y + s) % 4
        return pltpu.make_async_remote_copy(
            src_ref=low.at[j],
            dst_ref=whole.at[:, rows_of(ka), :],
            send_sem=send1.at[s],
            recv_sem=recv.at[ka],
            device_id=taker(j),
            device_id_type=MESH,
        )

    def chi_copy(s, slot):
        j = (y + s) % 4
        return pltpu.make_async_remote_copy(
            src_ref=chi_own.at[j],
            dst_ref=chi.at[slot],
            send_sem=send_chi.at[s],
            recv_sem=recv_chi.at[slot],
            device_id=taker(j),
            device_id_type=MESH,
        )

    def pass_on(piece, sem, target):
        block = whole.at[:, rows_of(piece), :]
        return pltpu.make_async_remote_copy(
            src_ref=block,
            dst_ref=block,
            send_sem=sem,
            recv_sem=recv.at[piece],
            device_id=target,
            device_id_type=MESH,
        )

    def pass_plane(piece, plane, sem, target):
        block = whole.at[plane, rows_of(piece), :]
        return pltpu.make_async_remote_copy(
            src_ref=block,
            dst_ref=block,
            send_sem=sem,
            recv_sem=recv.at[piece],
            device_id=target,
            device_id_type=MESH,
        )

    def piece_at(s, shift):
        return (1 - core) * 16 + (y + 4 - s) % 4 * 4 + (x + shift) % 4

    for s in range(4):
        copy1(s).start()
    for s in range(4):
        chi_copy(s, y).start()
    for i in range(2, 6):
        loads[i].start()

    for s in range(4):
        piece = piece_at(s, 0)
        pass_on(piece, send2.at[s, 0], right).wait_recv()
        pass_on(piece, send2.at[s, 0], right).start()
        pass_on(piece, send2.at[s, 1], left).start()
        pass_on(piece, send3.at[s, 0], partner).start()

    loads[2].wait()
    loads[3].wait()

    def select_rows(i, carry):
        at = pl.multiple_of(i * ROWS, ROWS)
        source = lax.broadcasted_iota(I32, (ROWS, K), 0) + at
        for c in range(2):
            selector[c, pl.ds(at, ROWS), :] = one_hot(source == cols_from[c:c + 1, :])
        return carry

    lax.fori_loop(0, K // ROWS, select_rows, 0)
    at_row = lax.broadcasted_iota(I32, (K, LANES), 0)
    at_lane = lax.broadcasted_iota(I32, (K, LANES), 1)
    by_ka = one_hot((at_lane % 32) == (at_row // 32))
    by_own = one_hot(((at_lane % 32) == (at_row % 32)) & ((at_row // 32) == ka))
    table_row = lax.broadcasted_iota(I32, (16, LANES), 0)
    table_lane = lax.broadcasted_iota(I32, (16, LANES), 1)
    for c in range(2):
        table = rows_from[c]
        owner = table // (QL * K) * 32 + table % K // ROWS
        local = table // K % QL * ROWS + table % ROWS
        wanted = jnp.where(owner == me, local + 1, 0).astype(F32).astype(BF16)
        wanted = jnp.dot(wanted, by_ka, preferred_element_type=F32)
        wanted = jnp.where(table_row // QL == table_lane // 32, wanted, 0.0)
        wanted = jnp.sum(wanted, axis=0, keepdims=True)
        local_row = (lax.broadcasted_iota(I32, (MINE, DEVS), 0) + 1).astype(F32)
        send_order[:, c * DEVS:(c + 1) * DEVS] = one_hot(local_row == wanted)
        owner = jnp.dot(owner.astype(F32).astype(BF16), by_own, preferred_element_type=F32)
        owner = jnp.where(table_row == pb * QL + table_lane // 32, owner, 0.0)
        owner = jnp.sum(owner, axis=0, keepdims=True)
        device = lax.broadcasted_iota(I32, (DEVS, MINE), 0).astype(F32)
        place_order[c] = one_hot(device == owner)

    for s in range(4):
        piece = piece_at(s, 3)
        pass_on(piece, send3.at[s, 1], partner).wait_recv()
        pass_plane(piece, 0, send2.at[s, 2], right).start()
        pass_on(piece, send3.at[s, 1], partner).start()
        piece = piece_at(s, 1)
        pass_on(piece, send3.at[s, 2], partner).wait_recv()
        pass_plane(piece, 1, send2.at[s, 3], left).start()
        pass_on(piece, send3.at[s, 2], partner).start()

    for s in range(4):
        chi_copy(s, s).wait_recv()

    def scaled(re, im, cols):
        chi_re, chi_im = chi[0, 0:1, cols], chi[0, 1:2, cols]
        return (re * chi_re - im * chi_im).astype(BF16), (re * chi_im + im * chi_re).astype(BF16)

    for j in range(4):
        at = j * ROWS
        rows = whole[:, rows_of((1 - core) * 16 + j * 4 + x), :]
        base[:, at:at + ROWS, :] = rows
        re, im = scaled(rows[0].astype(F32), rows[1].astype(F32), slice(0, K))
        left_even[at:at + ROWS, :] = re
        left_even[MINE + at:MINE + at + ROWS, :] = im

    for s in range(4):
        piece = piece_at(s, 2)
        pass_on(piece, send3.at[s, 3], partner).wait_recv()
        pass_on(piece, send3.at[s, 3], partner).start()
    for i in range(16):
        pass_on(core * 16 + i, send3.at[0, 0], partner).wait_recv()
    pl.semaphore_signal(known_half, inc=1, device_id=across, device_id_type=MESH)

    def product(left_op, n):
        cols = slice(n * NB, (n + 1) * NB)
        by_re = jnp.dot(left_op[...], whole[0, :, cols], preferred_element_type=F32)
        by_im = jnp.dot(left_op[...], whole[1, :, cols], preferred_element_type=F32)
        return by_re[:MINE] - by_im[MINE:], by_im[:MINE] + by_re[MINE:]

    def step(now, later):
        for n in range(K // NB):
            cols = slice(n * NB, (n + 1) * NB)
            re, im = product(now, n)
            re, im = scaled(base[0, :, cols].astype(F32) + re, base[1, :, cols].astype(F32) + im, cols)
            later[0:MINE, cols] = re
            later[MINE:2 * MINE, cols] = im

    def two_steps(i, carry):
        step(left_even, left_odd)
        step(left_odd, left_even)

        @pl.when(i == 0)
        def _():
            pl.semaphore_wait(known_half, 1)
            pl.semaphore_signal(known_all, inc=1, device_id=mirror, device_id_type=MESH)

        return carry

    lax.fori_loop(0, LADDER // 2 - 1, two_steps, 0)
    step(left_even, left_odd)

    def home_copy(h, s):
        j = (y + s) % 4
        return pltpu.make_async_remote_copy(
            src_ref=outgoing.at[h, j],
            dst_ref=home.at[h, y],
            send_sem=send_home.at[h, s],
            recv_sem=recv_home.at[h, y],
            device_id=giver(j),
            device_id_type=MESH,
        )

    def from_home(h, j):
        return pltpu.make_async_remote_copy(
            src_ref=outgoing.at[h, j],
            dst_ref=home.at[h, j],
            send_sem=send_home.at[h, j],
            recv_sem=recv_home.at[h, j],
            device_id=taker(j),
            device_id_type=MESH,
        )

    for n in range(K // NB):
        re, im = product(left_odd, n)
        h = n * NB // HALF
        cols = slice(n * NB % HALF, n * NB % HALF + NB)
        for j in range(4):
            outgoing[h, j, 0, :, cols] = re[j * ROWS:(j + 1) * ROWS].astype(BF16)
            outgoing[h, j, 1, :, cols] = im[j * ROWS:(j + 1) * ROWS].astype(BF16)
        if (n + 1) * NB % HALF == 0:
            for s in range(4):
                home_copy(h, s).start()

    for s in range(4):
        copy1(s).wait_send()
        chi_copy(s, s).wait_send()
        for t in range(2):
            pass_on(piece_at(s, 0), send2.at[s, t], right).wait_send()
        for t in range(2, 4):
            pass_plane(piece_at(s, 0), 0, send2.at[s, t], right).wait_send()
        for t in range(4):
            pass_on(piece_at(s, 0), send3.at[s, t], partner).wait_send()

    def row_copy(h, target):
        return pltpu.make_async_remote_copy(
            src_ref=packed.at[h, target],
            dst_ref=arrived.at[h, me],
            send_sem=send_row.at[h],
            recv_sem=recv_row.at[h],
            device_id=(target // 32, target % 32),
            device_id_type=MESH,
        )

    def own_copy(h):
        return pltpu.make_async_copy(packed.at[h, me], arrived.at[h, me], own_row.at[h])

    def others(h):
        return pltpu.make_async_remote_copy(
            src_ref=packed.at[h, pl.ds(0, DEVS - 1)],
            dst_ref=arrived.at[h, pl.ds(0, DEVS - 1)],
            send_sem=send_row.at[h],
            recv_sem=recv_row.at[h],
            device_id=right,
            device_id_type=MESH,
        )

    for h in range(2):
        for s in range(4):
            from_home(h, s).wait_recv()
        if h == 0:
            pl.semaphore_wait(known_all, 1)
        for p in range(2):
            rows = home[h, :, p].reshape(MINE, HALF)
            ordered = lax.dot_general(send_order[...], rows, OVER_ROWS, preferred_element_type=F32)
            for c in range(2):
                for b in range(BLOCKS):
                    stage[pl.ds((c * 2 + p) * BLOCKS + b, DEVS, stride=TILE), :] = ordered[
                        c * DEVS:(c + 1) * DEVS, b * LANES:(b + 1) * LANES
                    ]

        def pack(t, carry):
            packed[h, t] = stage[pl.ds(pl.multiple_of(t * TILE, TILE), TILE), :].astype(BF16)
            return carry

        lax.fori_loop(0, DEVS, pack, 0, unroll=8)

        def send(i, carry):
            row_copy(h, (me + i) % DEVS).start()
            return carry

        lax.fori_loop(1, DEVS, send, 0)
        own_copy(h).start()

    for h in range(2):
        for p in range(2):
            for q in range(QL):
                out_ref[p, q, :, h * HALF:(h + 1) * HALF] += home[h, q, p].astype(F32)

    stores = [
        pltpu.make_async_copy(source, target, store.at[i])
        for i, (source, target) in enumerate(((out_ref, to_ref), (out_a_ref, to_a_ref), (out_b_ref, to_b_ref)))
    ]
    stores[0].start()

    loads[4].wait()
    loads[5].wait()
    for h in range(2):
        others(h).wait_recv()
        own_copy(h).wait()

        def unpack(t, carry):
            stage[pl.ds(pl.multiple_of(t * TILE, TILE), TILE), :] = arrived[h, t].astype(F32)
            return carry

        lax.fori_loop(0, DEVS, unpack, 0, unroll=8)
        for b in range(4 * BLOCKS):
            lined_up[:, b * LANES:(b + 1) * LANES] = stage[pl.ds(b, DEVS, stride=TILE), :].astype(BF16)
        for c, sum_ref in enumerate((out_a_ref, out_b_ref)):
            for p in range(2):
                rows = lined_up[:, (c * 2 + p) * HALF:(c * 2 + p + 1) * HALF]
                placed[p * MINE:(p + 1) * MINE, :] = lax.dot_general(
                    place_order[c], rows, OVER_ROWS, preferred_element_type=F32
                ).astype(BF16)
            for n in range(K // NB):
                cols = slice(n * NB, (n + 1) * NB)
                moved = jnp.dot(
                    placed[...], selector[c, h * HALF:(h + 1) * HALF, cols], preferred_element_type=F32
                )
                sum_ref[:, :, :, cols] += moved.reshape(2, QL, ROWS, NB)
            if h == 1:
                stores[1 + c].start()

    for copy in stores:
        copy.wait()
    for h in range(2):
        others(h).wait_send()
        for s in range(4):
            home_copy(h, s).wait_send()


def run_ladder(vertex, cross_a, cross_b, bubble, row_maps, col_maps):
    out = jax.ShapeDtypeStruct(vertex.shape, F32)
    return pl.pallas_call(
        ladder_kernel,
        out_shape=(out, out, out),
        in_specs=[pl.BlockSpec(memory_space=pltpu.HBM)] * 6,
        out_specs=(pl.BlockSpec(memory_space=pltpu.HBM),) * 3,
        scratch_shapes=[
            pltpu.VMEM((2, QL, ROWS, K), F32),
            pltpu.VMEM((2, QL, ROWS, K), F32),
            pltpu.VMEM((2, QL, ROWS, K), F32),
            pltpu.VMEM((2, QL, K), F32),
            pltpu.VMEM((2, 4 * QL, K), I32),
            pltpu.VMEM((2, K), I32),
            pltpu.VMEM((QL, 2, ROWS, K), BF16),
            pltpu.VMEM((2, K, K), BF16),
            pltpu.VMEM((2, MINE, K), BF16),
            pltpu.VMEM((2 * MINE, K), BF16),
            pltpu.VMEM((2 * MINE, K), BF16),
            pltpu.VMEM((2, QL, 2, ROWS, HALF), BF16),
            pltpu.VMEM((2, QL, 2, ROWS, HALF), BF16),
            pltpu.VMEM((QL, 2, K), F32),
            pltpu.VMEM((QL, 2, K), F32),
            pltpu.VMEM((2, K, K), BF16),
            pltpu.VMEM((MINE, 2 * DEVS), BF16),
            pltpu.VMEM((2, DEVS, MINE), BF16),
            pltpu.VMEM((DEVS * TILE, LANES), F32),
            pltpu.VMEM((2, DEVS, TILE, LANES), BF16),
            pltpu.VMEM((2, DEVS, TILE, LANES), BF16),
            pltpu.VMEM((DEVS, 4 * HALF), BF16),
            pltpu.VMEM((2 * MINE, HALF), BF16),
            pltpu.SemaphoreType.DMA((6,)),
            pltpu.SemaphoreType.DMA((3,)),
            pltpu.SemaphoreType.DMA((4,)),
            pltpu.SemaphoreType.DMA((4,)),
            pltpu.SemaphoreType.DMA((4,)),
            pltpu.SemaphoreType.DMA((32,)),
            pltpu.SemaphoreType.DMA((4, 4)),
            pltpu.SemaphoreType.DMA((4, 4)),
            pltpu.SemaphoreType.DMA((2, 4)),
            pltpu.SemaphoreType.DMA((2, 4)),
            pltpu.SemaphoreType.DMA((2,)),
            pltpu.SemaphoreType.DMA((2,)),
            pltpu.SemaphoreType.DMA((2,)),
            pltpu.SemaphoreType.REGULAR,
            pltpu.SemaphoreType.REGULAR,
        ],
        compiler_params=pltpu.CompilerParams(
            collective_id=0, has_side_effects=True, vmem_limit_bytes=60 * 2**20
        ),
    )(vertex, cross_a, cross_b, bubble, row_maps, col_maps)


def hand_over_kernel(*refs):
    held, came, done = refs[6:]
    blocks = [(i, p, q) for i in range(3) for p in range(2) for q in range(0, QL, 2)]

    def bring(i, p, q):
        return pltpu.make_async_copy(refs[i].at[p, q:q + 2], held.at[i, p, q:q + 2], came.at[i, p, q])

    def write(i, p, q):
        return pltpu.make_async_copy(held.at[i, p, q:q + 2], refs[3 + i].at[p, q:q + 2], done.at[i, p, q])

    for block in blocks:
        bring(*block).start()
    for block in blocks:
        bring(*block).wait()
        write(*block).start()
    for block in blocks:
        write(*block).wait()


def per_device(*args):
    results = run_ladder(*args)
    shape = jax.ShapeDtypeStruct(args[0].shape, F32)
    return tuple(pl.pallas_call(
        hand_over_kernel,
        out_shape=(shape,) * 3,
        in_specs=[pl.BlockSpec(memory_space=pltpu.HBM)] * 3,
        out_specs=(pl.BlockSpec(memory_space=pltpu.HBM),) * 3,
        scratch_shapes=[
            pltpu.VMEM((3, 2, QL, ROWS, K), F32),
            pltpu.SemaphoreType.DMA((3, 2, QL)),
            pltpu.SemaphoreType.DMA((3, 2, QL)),
        ],
        compiler_params=pltpu.CompilerParams(vmem_limit_bytes=60 * 2**20),
    )(*results))


def solution(mesh):
    return jax.shard_map(
        per_device,
        mesh=mesh,
        in_specs=(
            P(None, "pb", "ka", None),
            P(None, "pb", "ka", None),
            P(None, "pb", "ka", None),
            P(None, "pb", None),
            P(),
            P(),
        ),
        out_specs=(P(None, "pb", "ka", None), P(None, "pb", "ka", None), P(None, "pb", "ka", None)),
        check_vma=False,
    )
```

```python
import jax
import jax.numpy as jnp
from jax import lax
from jax.experimental import pallas as pl
from jax.experimental.pallas import tpu as pltpu
from jax.sharding import PartitionSpec as P

LADDER = 6
MESH = pl.DeviceIdType.MESH
BF16 = jnp.bfloat16
F32 = jnp.float32
I32 = jnp.int32
K = 1024
ROWS = 32
QL = 4
MINE = QL * ROWS
NB = 256
DEVS = 128
LANES = 128
HALF = K // 2
TILE = 16
BLOCKS = HALF // LANES
OVER_ROWS = (((0,), (0,)), ((), ()))


def one_hot(hit):
    return jnp.where(hit, 1.0, 0.0).astype(BF16)


def ladder_kernel(
    vertex_ref, a_ref, b_ref, bubble_ref, row_ref, col_ref, to_ref, to_a_ref, to_b_ref,
    out_ref, out_a_ref, out_b_ref, bubble, rows_from, cols_from, low, whole, base, left_even, left_odd, outgoing, home, chi_own, chi, selector, send_order, place_order,
    stage, packed, arrived, lined_up, placed,
    load, store, send1, send_chi, recv_chi, recv, send2, send3, send_home, recv_home,
    send_row, recv_row, own_row, known_half, known_all,
):
    pb, ka = lax.axis_index("pb"), lax.axis_index("ka")
    z_hi, core = pb // 2, pb % 2
    z_lo, y, x = ka // 16, (ka // 4) % 4, ka % 4
    line = ka - x
    me = pb * 32 + ka

    def taker(j):
        return (z_hi * 2 + 1 - z_lo, core * 16 + j * 4 + x)

    def giver(j):
        return (z_hi * 2 + z_lo, (1 - core) * 16 + j * 4 + x)

    right = (pb, line + (x + 1) % 4)
    left = (pb, line + (x + 3) % 4)
    partner = (z_hi * 2 + 1 - core, ka)
    across = (pb, (ka + 16) % 32)
    mirror = ((pb + 2) % 4, ka)

    loads = [
        pltpu.make_async_copy(source, target, load.at[i])
        for i, (source, target) in enumerate((
            (vertex_ref, out_ref), (bubble_ref, bubble), (row_ref, rows_from), (col_ref, cols_from),
            (a_ref, out_a_ref), (b_ref, out_b_ref),
        ))
    ]
    loads[0].start()
    loads[1].start()
    barrier = pltpu.get_barrier_semaphore()
    for j in range(4):
        pl.semaphore_signal(barrier, inc=1, device_id=taker(j), device_id_type=MESH)
        pl.semaphore_signal(barrier, inc=1, device_id=giver(j), device_id_type=MESH)
    for other in (right, left, partner, across, mirror):
        pl.semaphore_signal(barrier, inc=1, device_id=other, device_id_type=MESH)
    loads[1].wait()
    for j in range(QL):
        chi_own[j] = bubble[:, j]
    loads[0].wait()
    for j in range(QL):
        low[j] = out_ref[:, j].astype(BF16)
    pl.semaphore_wait(barrier, 13)

    def rows_of(piece):
        return pl.ds(pl.multiple_of(piece * ROWS, ROWS), ROWS)

    def copy1(s, plane):
        j = (y + s) % 4
        return pltpu.make_async_remote_copy(
            src_ref=low.at[j, plane],
            dst_ref=whole.at[plane, rows_of(ka), :],
            send_sem=send1.at[s, plane],
            recv_sem=recv.at[plane, ka],
            device_id=taker(j),
            device_id_type=MESH,
        )

    def chi_copy(s, slot):
        j = (y + s) % 4
        return pltpu.make_async_remote_copy(
            src_ref=chi_own.at[j],
            dst_ref=chi.at[slot],
            send_sem=send_chi.at[s],
            recv_sem=recv_chi.at[slot],
            device_id=taker(j),
            device_id_type=MESH,
        )

    def pass_plane(piece, plane, sem, target):
        block = whole.at[plane, rows_of(piece), :]
        return pltpu.make_async_remote_copy(
            src_ref=block,
            dst_ref=block,
            send_sem=sem,
            recv_sem=recv.at[plane, piece],
            device_id=target,
            device_id_type=MESH,
        )

    def piece_at(s, shift):
        return (1 - core) * 16 + (y + 4 - s) % 4 * 4 + (x + shift) % 4

    for s in range(4):
        for plane in range(2):
            copy1(s, plane).start()
    for s in range(4):
        chi_copy(s, y).start()
    for i in range(2, 6):
        loads[i].start()

    def own_in(s):
        piece = piece_at(s, 0)
        for plane in range(2):
            pass_plane(piece, plane, send2.at[s, plane], right).wait_recv()
            pass_plane(piece, plane, send2.at[s, plane], right).start()
            pass_plane(piece, plane, send2.at[s, 2 + plane], left).start()
            pass_plane(piece, plane, send3.at[s, plane], partner).start()

    def from_sides(s):
        for plane in range(2):
            for side, target in ((3, right), (1, left)):
                piece = piece_at(s, side)
                slot = 2 + side - 1 + plane
                pass_plane(piece, plane, send3.at[s, slot], partner).wait_recv()
                if (plane == 0) == (side == 3):
                    pass_plane(piece, plane, send2.at[s, 4 + plane], target).start()
                pass_plane(piece, plane, send3.at[s, slot], partner).start()

    own_in(0)
    own_in(1)
    own_in(2)
    own_in(3)
    loads[2].wait()
    loads[3].wait()

    def select_rows(i, carry):
        at = pl.multiple_of(i * ROWS, ROWS)
        source = lax.broadcasted_iota(I32, (ROWS, K), 0) + at
        for c in range(2):
            selector[c, pl.ds(at, ROWS), :] = one_hot(source == cols_from[c:c + 1, :])
        return carry

    lax.fori_loop(0, K // ROWS, select_rows, 0)
    at_row = lax.broadcasted_iota(I32, (K, LANES), 0)
    at_lane = lax.broadcasted_iota(I32, (K, LANES), 1)
    by_ka = one_hot((at_lane % 32) == (at_row // 32))
    by_own = one_hot(((at_lane % 32) == (at_row % 32)) & ((at_row // 32) == ka))
    table_row = lax.broadcasted_iota(I32, (16, LANES), 0)
    table_lane = lax.broadcasted_iota(I32, (16, LANES), 1)
    for c in range(2):
        table = rows_from[c]
        owner = table // (QL * K) * 32 + table % K // ROWS
        local = table // K % QL * ROWS + table % ROWS
        wanted = jnp.where(owner == me, local + 1, 0).astype(F32).astype(BF16)
        wanted = jnp.dot(wanted, by_ka, preferred_element_type=F32)
        wanted = jnp.where(table_row // QL == table_lane // 32, wanted, 0.0)
        wanted = jnp.sum(wanted, axis=0, keepdims=True)
        local_row = (lax.broadcasted_iota(I32, (MINE, DEVS), 0) + 1).astype(F32)
        send_order[:, c * DEVS:(c + 1) * DEVS] = one_hot(local_row == wanted)
        owner = jnp.dot(owner.astype(F32).astype(BF16), by_own, preferred_element_type=F32)
        owner = jnp.where(table_row == pb * QL + table_lane // 32, owner, 0.0)
        owner = jnp.sum(owner, axis=0, keepdims=True)
        device = lax.broadcasted_iota(I32, (DEVS, MINE), 0).astype(F32)
        place_order[c] = one_hot(device == owner)

    from_sides(0)
    from_sides(1)
    from_sides(2)
    from_sides(3)

    for s in range(4):
        chi_copy(s, s).wait_recv()

    def scaled(re, im, cols):
        chi_re, chi_im = chi[0, 0:1, cols], chi[0, 1:2, cols]
        return (re * chi_re - im * chi_im).astype(BF16), (re * chi_im + im * chi_re).astype(BF16)

    for j in range(4):
        at = j * ROWS
        rows = whole[:, rows_of((1 - core) * 16 + j * 4 + x), :]
        base[:, at:at + ROWS, :] = rows
        re, im = scaled(rows[0].astype(F32), rows[1].astype(F32), slice(0, K))
        left_even[at:at + ROWS, :] = re
        left_even[MINE + at:MINE + at + ROWS, :] = im

    for s in range(4):
        for plane in range(2):
            piece = piece_at(s, 2)
            pass_plane(piece, plane, send3.at[s, 6 + plane], partner).wait_recv()
            pass_plane(piece, plane, send3.at[s, 6 + plane], partner).start()
    for i in range(16):
        for plane in range(2):
            pass_plane(core * 16 + i, plane, send3.at[0, 0], partner).wait_recv()
    pl.semaphore_signal(known_half, inc=1, device_id=across, device_id_type=MESH)

    def product(left_op, n):
        cols = slice(n * NB, (n + 1) * NB)
        by_re = jnp.dot(left_op[...], whole[0, :, cols], preferred_element_type=F32)
        by_im = jnp.dot(left_op[...], whole[1, :, cols], preferred_element_type=F32)
        return by_re[:MINE] - by_im[MINE:], by_im[:MINE] + by_re[MINE:]

    def step(now, later):
        for n in range(K // NB):
            cols = slice(n * NB, (n + 1) * NB)
            re, im = product(now, n)
            re, im = scaled(base[0, :, cols].astype(F32) + re, base[1, :, cols].astype(F32) + im, cols)
            later[0:MINE, cols] = re
            later[MINE:2 * MINE, cols] = im

    def two_steps(i, carry):
        step(left_even, left_odd)
        step(left_odd, left_even)

        @pl.when(i == 0)
        def _():
            pl.semaphore_wait(known_half, 1)
            pl.semaphore_signal(known_all, inc=1, device_id=mirror, device_id_type=MESH)

        return carry

    lax.fori_loop(0, LADDER // 2 - 1, two_steps, 0)
    step(left_even, left_odd)

    def home_copy(h, s):
        j = (y + s) % 4
        return pltpu.make_async_remote_copy(
            src_ref=outgoing.at[h, j],
            dst_ref=home.at[h, y],
            send_sem=send_home.at[h, s],
            recv_sem=recv_home.at[h, y],
            device_id=giver(j),
            device_id_type=MESH,
        )

    def from_home(h, j):
        return pltpu.make_async_remote_copy(
            src_ref=outgoing.at[h, j],
            dst_ref=home.at[h, j],
            send_sem=send_home.at[h, j],
            recv_sem=recv_home.at[h, j],
            device_id=taker(j),
            device_id_type=MESH,
        )

    for n in range(K // NB):
        re, im = product(left_odd, n)
        h = n * NB // HALF
        cols = slice(n * NB % HALF, n * NB % HALF + NB)
        for j in range(4):
            outgoing[h, j, 0, :, cols] = re[j * ROWS:(j + 1) * ROWS].astype(BF16)
            outgoing[h, j, 1, :, cols] = im[j * ROWS:(j + 1) * ROWS].astype(BF16)
        if (n + 1) * NB % HALF == 0:
            for s in range(4):
                home_copy(h, s).start()

    for s in range(4):
        chi_copy(s, s).wait_send()
        for plane in range(2):
            copy1(s, plane).wait_send()
        for t in range(6):
            pass_plane(piece_at(s, 0), 0, send2.at[s, t], right).wait_send()
        for t in range(8):
            pass_plane(piece_at(s, 0), 0, send3.at[s, t], partner).wait_send()

    def row_copy(h, target):
        return pltpu.make_async_remote_copy(
            src_ref=packed.at[h, target],
            dst_ref=arrived.at[h, me],
            send_sem=send_row.at[h],
            recv_sem=recv_row.at[h],
            device_id=(target // 32, target % 32),
            device_id_type=MESH,
        )

    def own_copy(h):
        return pltpu.make_async_copy(packed.at[h, me], arrived.at[h, me], own_row.at[h])

    def others(h):
        return pltpu.make_async_remote_copy(
            src_ref=packed.at[h, pl.ds(0, DEVS - 1)],
            dst_ref=arrived.at[h, pl.ds(0, DEVS - 1)],
            send_sem=send_row.at[h],
            recv_sem=recv_row.at[h],
            device_id=right,
            device_id_type=MESH,
        )

    for h in range(2):
        for s in range(4):
            from_home(h, s).wait_recv()
        if h == 0:
            pl.semaphore_wait(known_all, 1)
        for p in range(2):
            rows = home[h, :, p].reshape(MINE, HALF)
            ordered = lax.dot_general(send_order[...], rows, OVER_ROWS, preferred_element_type=F32)
            for c in range(2):
                for b in range(BLOCKS):
                    stage[pl.ds((c * 2 + p) * BLOCKS + b, DEVS, stride=TILE), :] = ordered[
                        c * DEVS:(c + 1) * DEVS, b * LANES:(b + 1) * LANES
                    ]

        def pack(t, carry):
            packed[h, t] = stage[pl.ds(pl.multiple_of(t * TILE, TILE), TILE), :].astype(BF16)
            return carry

        lax.fori_loop(0, DEVS, pack, 0, unroll=8)

        def send(i, carry):
            row_copy(h, (me + i) % DEVS).start()
            return carry

        lax.fori_loop(1, DEVS, send, 0)
        own_copy(h).start()

    for h in range(2):
        for p in range(2):
            for q in range(QL):
                out_ref[p, q, :, h * HALF:(h + 1) * HALF] += home[h, q, p].astype(F32)

    stores = [
        pltpu.make_async_copy(source, target, store.at[i])
        for i, (source, target) in enumerate(((out_ref, to_ref), (out_a_ref, to_a_ref), (out_b_ref, to_b_ref)))
    ]
    stores[0].start()

    loads[4].wait()
    loads[5].wait()
    for h in range(2):
        others(h).wait_recv()
        own_copy(h).wait()

        def unpack(t, carry):
            stage[pl.ds(pl.multiple_of(t * TILE, TILE), TILE), :] = arrived[h, t].astype(F32)
            return carry

        lax.fori_loop(0, DEVS, unpack, 0, unroll=8)
        for b in range(4 * BLOCKS):
            lined_up[:, b * LANES:(b + 1) * LANES] = stage[pl.ds(b, DEVS, stride=TILE), :].astype(BF16)
        for c, sum_ref in enumerate((out_a_ref, out_b_ref)):
            for p in range(2):
                rows = lined_up[:, (c * 2 + p) * HALF:(c * 2 + p + 1) * HALF]
                placed[p * MINE:(p + 1) * MINE, :] = lax.dot_general(
                    place_order[c], rows, OVER_ROWS, preferred_element_type=F32
                ).astype(BF16)
            for n in range(K // NB):
                cols = slice(n * NB, (n + 1) * NB)
                moved = jnp.dot(
                    placed[...], selector[c, h * HALF:(h + 1) * HALF, cols], preferred_element_type=F32
                )
                sum_ref[:, :, :, cols] += moved.reshape(2, QL, ROWS, NB)
            if h == 1:
                stores[1 + c].start()

    for copy in stores:
        copy.wait()
    for h in range(2):
        others(h).wait_send()
        for s in range(4):
            home_copy(h, s).wait_send()


def run_ladder(vertex, cross_a, cross_b, bubble, row_maps, col_maps):
    out = jax.ShapeDtypeStruct(vertex.shape, F32)
    return pl.pallas_call(
        ladder_kernel,
        out_shape=(out, out, out),
        in_specs=[pl.BlockSpec(memory_space=pltpu.HBM)] * 6,
        out_specs=(pl.BlockSpec(memory_space=pltpu.HBM),) * 3,
        scratch_shapes=[
            pltpu.VMEM((2, QL, ROWS, K), F32),
            pltpu.VMEM((2, QL, ROWS, K), F32),
            pltpu.VMEM((2, QL, ROWS, K), F32),
            pltpu.VMEM((2, QL, K), F32),
            pltpu.VMEM((2, 4 * QL, K), I32),
            pltpu.VMEM((2, K), I32),
            pltpu.VMEM((QL, 2, ROWS, K), BF16),
            pltpu.VMEM((2, K, K), BF16),
            pltpu.VMEM((2, MINE, K), BF16),
            pltpu.VMEM((2 * MINE, K), BF16),
            pltpu.VMEM((2 * MINE, K), BF16),
            pltpu.VMEM((2, QL, 2, ROWS, HALF), BF16),
            pltpu.VMEM((2, QL, 2, ROWS, HALF), BF16),
            pltpu.VMEM((QL, 2, K), F32),
            pltpu.VMEM((QL, 2, K), F32),
            pltpu.VMEM((2, K, K), BF16),
            pltpu.VMEM((MINE, 2 * DEVS), BF16),
            pltpu.VMEM((2, DEVS, MINE), BF16),
            pltpu.VMEM((DEVS * TILE, LANES), F32),
            pltpu.VMEM((2, DEVS, TILE, LANES), BF16),
            pltpu.VMEM((2, DEVS, TILE, LANES), BF16),
            pltpu.VMEM((DEVS, 4 * HALF), BF16),
            pltpu.VMEM((2 * MINE, HALF), BF16),
            pltpu.SemaphoreType.DMA((6,)),
            pltpu.SemaphoreType.DMA((3,)),
            pltpu.SemaphoreType.DMA((4, 2)),
            pltpu.SemaphoreType.DMA((4,)),
            pltpu.SemaphoreType.DMA((4,)),
            pltpu.SemaphoreType.DMA((2, 32)),
            pltpu.SemaphoreType.DMA((4, 6)),
            pltpu.SemaphoreType.DMA((4, 8)),
            pltpu.SemaphoreType.DMA((2, 4)),
            pltpu.SemaphoreType.DMA((2, 4)),
            pltpu.SemaphoreType.DMA((2,)),
            pltpu.SemaphoreType.DMA((2,)),
            pltpu.SemaphoreType.DMA((2,)),
            pltpu.SemaphoreType.REGULAR,
            pltpu.SemaphoreType.REGULAR,
        ],
        compiler_params=pltpu.CompilerParams(
            collective_id=0, has_side_effects=True, vmem_limit_bytes=60 * 2**20
        ),
    )(vertex, cross_a, cross_b, bubble, row_maps, col_maps)


def hand_over_kernel(*refs):
    held, came, done = refs[6:]
    blocks = [(i, p, q) for i in range(3) for p in range(2) for q in range(0, QL, 2)]

    def bring(i, p, q):
        return pltpu.make_async_copy(refs[i].at[p, q:q + 2], held.at[i, p, q:q + 2], came.at[i, p, q])

    def write(i, p, q):
        return pltpu.make_async_copy(held.at[i, p, q:q + 2], refs[3 + i].at[p, q:q + 2], done.at[i, p, q])

    for block in blocks:
        bring(*block).start()
    for block in blocks:
        bring(*block).wait()
        write(*block).start()
    for block in blocks:
        write(*block).wait()


def per_device(*args):
    results = run_ladder(*args)
    shape = jax.ShapeDtypeStruct(args[0].shape, F32)
    return tuple(pl.pallas_call(
        hand_over_kernel,
        out_shape=(shape,) * 3,
        in_specs=[pl.BlockSpec(memory_space=pltpu.HBM)] * 3,
        out_specs=(pl.BlockSpec(memory_space=pltpu.HBM),) * 3,
        scratch_shapes=[
            pltpu.VMEM((3, 2, QL, ROWS, K), F32),
            pltpu.SemaphoreType.DMA((3, 2, QL)),
            pltpu.SemaphoreType.DMA((3, 2, QL)),
        ],
        compiler_params=pltpu.CompilerParams(vmem_limit_bytes=60 * 2**20),
    )(*results))


def solution(mesh):
    return jax.shard_map(
        per_device,
        mesh=mesh,
        in_specs=(
            P(None, "pb", "ka", None),
            P(None, "pb", "ka", None),
            P(None, "pb", "ka", None),
            P(None, "pb", None),
            P(),
            P(),
        ),
        out_specs=(P(None, "pb", "ka", None), P(None, "pb", "ka", None), P(None, "pb", "ka", None)),
        check_vma=False,
    )
```

```python
import jax
import jax.numpy as jnp
from jax import lax
from jax.experimental import pallas as pl
from jax.experimental.pallas import tpu as pltpu
from jax.sharding import PartitionSpec as P

LADDER = 6
MESH = pl.DeviceIdType.MESH
BF16 = jnp.bfloat16
F32 = jnp.float32
I32 = jnp.int32
K = 1024
ROWS = 32
QL = 4
MINE = QL * ROWS
NB = 256
DEVS = 128
LANES = 128
HALF = K // 2
TILE = 16
BLOCKS = HALF // LANES
OVER_ROWS = (((0,), (0,)), ((), ()))


def one_hot(hit):
    return jnp.where(hit, 1.0, 0.0).astype(BF16)


def ladder_kernel(
    vertex_ref, low, a_ref, b_ref, bubble, rows_from, cols_from, out_ref, out_a_ref, out_b_ref,
    whole, base, left_even, left_odd, outgoing, home, chi_own, chi, selector, send_order, place_order,
    stage, packed, arrived, lined_up, placed,
    load, send1, send_chi, recv_chi, recv, send2, send3, send_home, recv_home,
    send_row, recv_row, own_row, known_half, known_all,
):
    pb, ka = lax.axis_index("pb"), lax.axis_index("ka")
    z_hi, core = pb // 2, pb % 2
    z_lo, y, x = ka // 16, (ka // 4) % 4, ka % 4
    line = ka - x
    me = pb * 32 + ka

    def taker(j):
        return (z_hi * 2 + 1 - z_lo, core * 16 + j * 4 + x)

    def giver(j):
        return (z_hi * 2 + z_lo, (1 - core) * 16 + j * 4 + x)

    right = (pb, line + (x + 1) % 4)
    left = (pb, line + (x + 3) % 4)
    partner = (z_hi * 2 + 1 - core, ka)
    across = (pb, (ka + 16) % 32)
    mirror = ((pb + 2) % 4, ka)

    loads = [
        pltpu.make_async_copy(source, target, load.at[i])
        for i, (source, target) in enumerate(((vertex_ref, out_ref), (a_ref, out_a_ref), (b_ref, out_b_ref)))
    ]
    barrier = pltpu.get_barrier_semaphore()
    for j in range(4):
        pl.semaphore_signal(barrier, inc=1, device_id=taker(j), device_id_type=MESH)
        pl.semaphore_signal(barrier, inc=1, device_id=giver(j), device_id_type=MESH)
    for other in (right, left, partner, across, mirror):
        pl.semaphore_signal(barrier, inc=1, device_id=other, device_id_type=MESH)
    for j in range(QL):
        chi_own[j] = bubble[:, j]
    pl.semaphore_wait(barrier, 13)

    def rows_of(piece):
        return pl.ds(pl.multiple_of(piece * ROWS, ROWS), ROWS)

    def copy1(s, plane):
        j = (y + s) % 4
        return pltpu.make_async_remote_copy(
            src_ref=low.at[plane, j],
            dst_ref=whole.at[plane, rows_of(ka), :],
            send_sem=send1.at[s, plane],
            recv_sem=recv.at[plane, ka],
            device_id=taker(j),
            device_id_type=MESH,
        )

    def chi_copy(s, slot):
        j = (y + s) % 4
        return pltpu.make_async_remote_copy(
            src_ref=chi_own.at[j],
            dst_ref=chi.at[slot],
            send_sem=send_chi.at[s],
            recv_sem=recv_chi.at[slot],
            device_id=taker(j),
            device_id_type=MESH,
        )

    def pass_plane(piece, plane, sem, target):
        block = whole.at[plane, rows_of(piece), :]
        return pltpu.make_async_remote_copy(
            src_ref=block,
            dst_ref=block,
            send_sem=sem,
            recv_sem=recv.at[plane, piece],
            device_id=target,
            device_id_type=MESH,
        )

    def piece_at(s, shift):
        return (1 - core) * 16 + (y + 4 - s) % 4 * 4 + (x + shift) % 4

    for s in range(4):
        for plane in range(2):
            copy1(s, plane).start()
    for s in range(4):
        chi_copy(s, y).start()
    for copy in loads:
        copy.start()

    def own_in(s):
        piece = piece_at(s, 0)
        for plane in range(2):
            pass_plane(piece, plane, send2.at[s, plane], right).wait_recv()
            pass_plane(piece, plane, send2.at[s, plane], right).start()
            pass_plane(piece, plane, send2.at[s, 2 + plane], left).start()
            pass_plane(piece, plane, send3.at[s, plane], partner).start()

    def from_sides(s):
        for plane in range(2):
            for side, target in ((3, right), (1, left)):
                piece = piece_at(s, side)
                slot = 2 + side - 1 + plane
                pass_plane(piece, plane, send3.at[s, slot], partner).wait_recv()
                if (plane == 0) == (side == 3):
                    pass_plane(piece, plane, send2.at[s, 4 + plane], target).start()
                pass_plane(piece, plane, send3.at[s, slot], partner).start()

    own_in(0)
    own_in(1)
    own_in(2)
    own_in(3)

    def select_rows(i, carry):
        at = pl.multiple_of(i * ROWS, ROWS)
        source = lax.broadcasted_iota(I32, (ROWS, K), 0) + at
        for c in range(2):
            selector[c, pl.ds(at, ROWS), :] = one_hot(source == cols_from[c:c + 1, :])
        return carry

    lax.fori_loop(0, K // ROWS, select_rows, 0)
    at_row = lax.broadcasted_iota(I32, (K, LANES), 0)
    at_lane = lax.broadcasted_iota(I32, (K, LANES), 1)
    by_ka = one_hot((at_lane % 32) == (at_row // 32))
    by_own = one_hot(((at_lane % 32) == (at_row % 32)) & ((at_row // 32) == ka))
    table_row = lax.broadcasted_iota(I32, (16, LANES), 0)
    table_lane = lax.broadcasted_iota(I32, (16, LANES), 1)
    for c in range(2):
        table = rows_from[c]
        owner = table // (QL * K) * 32 + table % K // ROWS
        local = table // K % QL * ROWS + table % ROWS
        wanted = jnp.where(owner == me, local + 1, 0).astype(F32).astype(BF16)
        wanted = jnp.dot(wanted, by_ka, preferred_element_type=F32)
        wanted = jnp.where(table_row // QL == table_lane // 32, wanted, 0.0)
        wanted = jnp.sum(wanted, axis=0, keepdims=True)
        local_row = (lax.broadcasted_iota(I32, (MINE, DEVS), 0) + 1).astype(F32)
        send_order[:, c * DEVS:(c + 1) * DEVS] = one_hot(local_row == wanted)
        owner = jnp.dot(owner.astype(F32).astype(BF16), by_own, preferred_element_type=F32)
        owner = jnp.where(table_row == pb * QL + table_lane // 32, owner, 0.0)
        owner = jnp.sum(owner, axis=0, keepdims=True)
        device = lax.broadcasted_iota(I32, (DEVS, MINE), 0).astype(F32)
        place_order[c] = one_hot(device == owner)

    from_sides(0)
    from_sides(1)
    from_sides(2)
    from_sides(3)

    for s in range(4):
        chi_copy(s, s).wait_recv()

    def scaled(re, im, cols):
        chi_re, chi_im = chi[0, 0:1, cols], chi[0, 1:2, cols]
        return (re * chi_re - im * chi_im).astype(BF16), (re * chi_im + im * chi_re).astype(BF16)

    for j in range(4):
        at = j * ROWS
        rows = whole[:, rows_of((1 - core) * 16 + j * 4 + x), :]
        base[:, at:at + ROWS, :] = rows
        re, im = scaled(rows[0].astype(F32), rows[1].astype(F32), slice(0, K))
        left_even[at:at + ROWS, :] = re
        left_even[MINE + at:MINE + at + ROWS, :] = im

    for s in range(4):
        for plane in range(2):
            piece = piece_at(s, 2)
            pass_plane(piece, plane, send3.at[s, 6 + plane], partner).wait_recv()
            pass_plane(piece, plane, send3.at[s, 6 + plane], partner).start()
    for i in range(16):
        for plane in range(2):
            pass_plane(core * 16 + i, plane, send3.at[0, 0], partner).wait_recv()
    pl.semaphore_signal(known_half, inc=1, device_id=across, device_id_type=MESH)

    def product(left_op, n):
        cols = slice(n * NB, (n + 1) * NB)
        by_re = jnp.dot(left_op[...], whole[0, :, cols], preferred_element_type=F32)
        by_im = jnp.dot(left_op[...], whole[1, :, cols], preferred_element_type=F32)
        return by_re[:MINE] - by_im[MINE:], by_im[:MINE] + by_re[MINE:]

    def step(now, later):
        for n in range(K // NB):
            cols = slice(n * NB, (n + 1) * NB)
            re, im = product(now, n)
            re, im = scaled(base[0, :, cols].astype(F32) + re, base[1, :, cols].astype(F32) + im, cols)
            later[0:MINE, cols] = re
            later[MINE:2 * MINE, cols] = im

    def two_steps(i, carry):
        step(left_even, left_odd)
        step(left_odd, left_even)

        @pl.when(i == 0)
        def _():
            pl.semaphore_wait(known_half, 1)
            pl.semaphore_signal(known_all, inc=1, device_id=mirror, device_id_type=MESH)

        return carry

    lax.fori_loop(0, LADDER // 2 - 1, two_steps, 0)
    step(left_even, left_odd)

    def home_copy(h, s):
        j = (y + s) % 4
        return pltpu.make_async_remote_copy(
            src_ref=outgoing.at[h, j],
            dst_ref=home.at[h, y],
            send_sem=send_home.at[h, s],
            recv_sem=recv_home.at[h, y],
            device_id=giver(j),
            device_id_type=MESH,
        )

    def from_home(h, j):
        return pltpu.make_async_remote_copy(
            src_ref=outgoing.at[h, j],
            dst_ref=home.at[h, j],
            send_sem=send_home.at[h, j],
            recv_sem=recv_home.at[h, j],
            device_id=taker(j),
            device_id_type=MESH,
        )

    for n in range(K // NB):
        re, im = product(left_odd, n)
        h = n * NB // HALF
        cols = slice(n * NB % HALF, n * NB % HALF + NB)
        for j in range(4):
            outgoing[h, j, 0, :, cols] = re[j * ROWS:(j + 1) * ROWS].astype(BF16)
            outgoing[h, j, 1, :, cols] = im[j * ROWS:(j + 1) * ROWS].astype(BF16)
        if (n + 1) * NB % HALF == 0:
            for s in range(4):
                home_copy(h, s).start()

    for s in range(4):
        chi_copy(s, s).wait_send()
        for plane in range(2):
            copy1(s, plane).wait_send()
        for t in range(6):
            pass_plane(piece_at(s, 0), 0, send2.at[s, t], right).wait_send()
        for t in range(8):
            pass_plane(piece_at(s, 0), 0, send3.at[s, t], partner).wait_send()

    def row_copy(h, target):
        return pltpu.make_async_remote_copy(
            src_ref=packed.at[h, target],
            dst_ref=arrived.at[h, me],
            send_sem=send_row.at[h],
            recv_sem=recv_row.at[h],
            device_id=(target // 32, target % 32),
            device_id_type=MESH,
        )

    def own_copy(h):
        return pltpu.make_async_copy(packed.at[h, me], arrived.at[h, me], own_row.at[h])

    def others(h):
        return pltpu.make_async_remote_copy(
            src_ref=packed.at[h, pl.ds(0, DEVS - 1)],
            dst_ref=arrived.at[h, pl.ds(0, DEVS - 1)],
            send_sem=send_row.at[h],
            recv_sem=recv_row.at[h],
            device_id=right,
            device_id_type=MESH,
        )

    for h in range(2):
        for s in range(4):
            from_home(h, s).wait_recv()
        if h == 0:
            pl.semaphore_wait(known_all, 1)
        for p in range(2):
            rows = home[h, :, p].reshape(MINE, HALF)
            ordered = lax.dot_general(send_order[...], rows, OVER_ROWS, preferred_element_type=F32)
            for c in range(2):
                for b in range(BLOCKS):
                    stage[pl.ds((c * 2 + p) * BLOCKS + b, DEVS, stride=TILE), :] = ordered[
                        c * DEVS:(c + 1) * DEVS, b * LANES:(b + 1) * LANES
                    ]

        def pack(t, carry):
            packed[h, t] = stage[pl.ds(pl.multiple_of(t * TILE, TILE), TILE), :].astype(BF16)
            return carry

        lax.fori_loop(0, DEVS, pack, 0, unroll=8)

        def send(i, carry):
            row_copy(h, (me + i) % DEVS).start()
            return carry

        lax.fori_loop(1, DEVS, send, 0)
        own_copy(h).start()

    for copy in loads:
        copy.wait()
    for h in range(2):
        for p in range(2):
            for q in range(QL):
                out_ref[p, q, :, h * HALF:(h + 1) * HALF] += home[h, q, p].astype(F32)

    for h in range(2):
        others(h).wait_recv()
        own_copy(h).wait()

        def unpack(t, carry):
            stage[pl.ds(pl.multiple_of(t * TILE, TILE), TILE), :] = arrived[h, t].astype(F32)
            return carry

        lax.fori_loop(0, DEVS, unpack, 0, unroll=8)
        for b in range(4 * BLOCKS):
            lined_up[:, b * LANES:(b + 1) * LANES] = stage[pl.ds(b, DEVS, stride=TILE), :].astype(BF16)
        for c, sum_ref in enumerate((out_a_ref, out_b_ref)):
            for p in range(2):
                rows = lined_up[:, (c * 2 + p) * HALF:(c * 2 + p + 1) * HALF]
                placed[p * MINE:(p + 1) * MINE, :] = lax.dot_general(
                    place_order[c], rows, OVER_ROWS, preferred_element_type=F32
                ).astype(BF16)
            for n in range(K // NB):
                cols = slice(n * NB, (n + 1) * NB)
                moved = jnp.dot(
                    placed[...], selector[c, h * HALF:(h + 1) * HALF, cols], preferred_element_type=F32
                )
                sum_ref[:, :, :, cols] += moved.reshape(2, QL, ROWS, NB)

    for h in range(2):
        others(h).wait_send()
        for s in range(4):
            home_copy(h, s).wait_send()


def run_ladder(vertex, cross_a, cross_b, bubble, row_maps, col_maps):
    out = jax.ShapeDtypeStruct(vertex.shape, F32)
    hbm, vmem = pl.BlockSpec(memory_space=pltpu.HBM), pl.BlockSpec(memory_space=pltpu.VMEM)
    return pl.pallas_call(
        ladder_kernel,
        out_shape=(out, out, out),
        in_specs=[hbm, vmem, hbm, hbm, vmem, vmem, vmem],
        out_specs=(vmem, vmem, vmem),
        scratch_shapes=[
            pltpu.VMEM((2, K, K), BF16),
            pltpu.VMEM((2, MINE, K), BF16),
            pltpu.VMEM((2 * MINE, K), BF16),
            pltpu.VMEM((2 * MINE, K), BF16),
            pltpu.VMEM((2, QL, 2, ROWS, HALF), BF16),
            pltpu.VMEM((2, QL, 2, ROWS, HALF), BF16),
            pltpu.VMEM((QL, 2, K), F32),
            pltpu.VMEM((QL, 2, K), F32),
            pltpu.VMEM((2, K, K), BF16),
            pltpu.VMEM((MINE, 2 * DEVS), BF16),
            pltpu.VMEM((2, DEVS, MINE), BF16),
            pltpu.VMEM((DEVS * TILE, LANES), F32),
            pltpu.VMEM((2, DEVS, TILE, LANES), BF16),
            pltpu.VMEM((2, DEVS, TILE, LANES), BF16),
            pltpu.VMEM((DEVS, 4 * HALF), BF16),
            pltpu.VMEM((2 * MINE, HALF), BF16),
            pltpu.SemaphoreType.DMA((3,)),
            pltpu.SemaphoreType.DMA((4, 2)),
            pltpu.SemaphoreType.DMA((4,)),
            pltpu.SemaphoreType.DMA((4,)),
            pltpu.SemaphoreType.DMA((2, 32)),
            pltpu.SemaphoreType.DMA((4, 6)),
            pltpu.SemaphoreType.DMA((4, 8)),
            pltpu.SemaphoreType.DMA((2, 4)),
            pltpu.SemaphoreType.DMA((2, 4)),
            pltpu.SemaphoreType.DMA((2,)),
            pltpu.SemaphoreType.DMA((2,)),
            pltpu.SemaphoreType.DMA((2,)),
            pltpu.SemaphoreType.REGULAR,
            pltpu.SemaphoreType.REGULAR,
        ],
        compiler_params=pltpu.CompilerParams(
            collective_id=0, has_side_effects=True, vmem_limit_bytes=50 * 2**20
        ),
    )(vertex, vertex.astype(BF16), cross_a, cross_b, bubble, row_maps, col_maps)


def hand_over_kernel(*refs):
    done = refs[-1]
    copies = [
        pltpu.make_async_copy(refs[i].at[p], refs[3 + i].at[p], done.at[i, p])
        for i in range(3) for p in range(2)
    ]
    for copy in copies:
        copy.start()
    for copy in copies:
        copy.wait()


def per_device(*args):
    results = run_ladder(*args)
    shape = jax.ShapeDtypeStruct(args[0].shape, F32)
    return tuple(pl.pallas_call(
        hand_over_kernel,
        out_shape=(shape,) * 3,
        in_specs=[pl.BlockSpec(memory_space=pltpu.VMEM)] * 3,
        out_specs=(pl.BlockSpec(memory_space=pltpu.HBM),) * 3,
        scratch_shapes=[pltpu.SemaphoreType.DMA((3, 2))],
        compiler_params=pltpu.CompilerParams(vmem_limit_bytes=50 * 2**20),
    )(*results))


def solution(mesh):
    return jax.shard_map(
        per_device,
        mesh=mesh,
        in_specs=(
            P(None, "pb", "ka", None),
            P(None, "pb", "ka", None),
            P(None, "pb", "ka", None),
            P(None, "pb", None),
            P(),
            P(),
        ),
        out_specs=(P(None, "pb", "ka", None), P(None, "pb", "ka", None), P(None, "pb", "ka", None)),
        check_vma=False,
    )
```

```python
import jax
import jax.numpy as jnp
from jax import lax
from jax.experimental import pallas as pl
from jax.experimental.pallas import tpu as pltpu
from jax.sharding import PartitionSpec as P

LADDER = 6
MESH = pl.DeviceIdType.MESH
BF16 = jnp.bfloat16
F32 = jnp.float32
I32 = jnp.int32
K = 1024
ROWS = 32
QL = 4
MINE = QL * ROWS
NB = 256
DEVS = 128
LANES = 128
HALF = K // 2
TILE = 16
BLOCKS = HALF // LANES
OVER_ROWS = (((0,), (0,)), ((), ()))


def one_hot(hit):
    return jnp.where(hit, 1.0, 0.0).astype(BF16)


def ladder_kernel(
    vertex_ref, low, a_ref, b_ref, bubble, rows_from, cols_from, out_ref, out_a_ref, out_b_ref,
    whole, base, left_even, left_odd, outgoing, home, chi_own, chi, selector, send_order, place_order,
    stage, packed, arrived, lined_up, placed,
    load, send1, send_chi, recv_chi, recv, send2, send3, send_home, recv_home,
    send_row, recv_row, own_row, known_half, known_all,
):
    pb, ka = lax.axis_index("pb"), lax.axis_index("ka")
    z_hi, core = pb // 2, pb % 2
    z_lo, y, x = ka // 16, (ka // 4) % 4, ka % 4
    line = ka - x
    me = pb * 32 + ka

    def taker(j):
        return (z_hi * 2 + 1 - z_lo, core * 16 + j * 4 + x)

    def giver(j):
        return (z_hi * 2 + z_lo, (1 - core) * 16 + j * 4 + x)

    right = (pb, line + (x + 1) % 4)
    left = (pb, line + (x + 3) % 4)
    partner = (z_hi * 2 + 1 - core, ka)
    across = (pb, (ka + 16) % 32)
    mirror = ((pb + 2) % 4, ka)

    loads = [
        pltpu.make_async_copy(source, target, load.at[i])
        for i, (source, target) in enumerate(((vertex_ref, out_ref), (a_ref, out_a_ref), (b_ref, out_b_ref)))
    ]
    barrier = pltpu.get_barrier_semaphore()
    for j in range(4):
        pl.semaphore_signal(barrier, inc=1, device_id=taker(j), device_id_type=MESH)
        pl.semaphore_signal(barrier, inc=1, device_id=giver(j), device_id_type=MESH)
    for other in (right, left, partner, across, mirror):
        pl.semaphore_signal(barrier, inc=1, device_id=other, device_id_type=MESH)
    for j in range(QL):
        chi_own[j] = bubble[:, j]
    pl.semaphore_wait(barrier, 13)

    def rows_of(piece):
        return pl.ds(pl.multiple_of(piece * ROWS, ROWS), ROWS)

    def copy1(s, plane):
        j = (y + s) % 4
        return pltpu.make_async_remote_copy(
            src_ref=low.at[plane, j],
            dst_ref=whole.at[plane, rows_of(ka), :],
            send_sem=send1.at[s, plane],
            recv_sem=recv.at[plane, ka],
            device_id=taker(j),
            device_id_type=MESH,
        )

    def chi_copy(s, slot):
        j = (y + s) % 4
        return pltpu.make_async_remote_copy(
            src_ref=chi_own.at[j],
            dst_ref=chi.at[slot],
            send_sem=send_chi.at[s],
            recv_sem=recv_chi.at[slot],
            device_id=taker(j),
            device_id_type=MESH,
        )

    def pass_plane(piece, plane, sem, target):
        block = whole.at[plane, rows_of(piece), :]
        return pltpu.make_async_remote_copy(
            src_ref=block,
            dst_ref=block,
            send_sem=sem,
            recv_sem=recv.at[plane, piece],
            device_id=target,
            device_id_type=MESH,
        )

    def piece_at(s, shift):
        return (1 - core) * 16 + (y + 4 - s) % 4 * 4 + (x + shift) % 4

    for s in range(4):
        for plane in range(2):
            copy1(s, plane).start()
    for s in range(4):
        chi_copy(s, y).start()
    for copy in loads:
        copy.start()

    def own_in(s):
        piece = piece_at(s, 0)
        for plane in range(2):
            pass_plane(piece, plane, send2.at[s, plane], right).wait_recv()
            pass_plane(piece, plane, send2.at[s, plane], right).start()
            pass_plane(piece, plane, send2.at[s, 2 + plane], left).start()
            pass_plane(piece, plane, send3.at[s, plane], partner).start()

    def from_sides(s):
        for plane in range(2):
            for side, target in ((3, right), (1, left)):
                piece = piece_at(s, side)
                slot = 2 + side - 1 + plane
                pass_plane(piece, plane, send3.at[s, slot], partner).wait_recv()
                if (plane == 0) == (side == 3):
                    pass_plane(piece, plane, send2.at[s, 4 + plane], target).start()
                pass_plane(piece, plane, send3.at[s, slot], partner).start()

    def select_rows(i, carry):
        at = pl.multiple_of(i * ROWS, ROWS)
        source = lax.broadcasted_iota(I32, (ROWS, K), 0) + at
        for c in range(2):
            selector[c, pl.ds(at, ROWS), :] = one_hot(source == cols_from[c:c + 1, :])
        return carry

    lax.fori_loop(0, K // ROWS, select_rows, 0)
    at_row = lax.broadcasted_iota(I32, (K, LANES), 0)
    at_lane = lax.broadcasted_iota(I32, (K, LANES), 1)
    by_ka = one_hot((at_lane % 32) == (at_row // 32))
    by_own = one_hot(((at_lane % 32) == (at_row % 32)) & ((at_row // 32) == ka))
    table_row = lax.broadcasted_iota(I32, (16, LANES), 0)
    table_lane = lax.broadcasted_iota(I32, (16, LANES), 1)
    for c in range(2):
        table = rows_from[c]
        owner = table // (QL * K) * 32 + table % K // ROWS
        local = table // K % QL * ROWS + table % ROWS
        wanted = jnp.where(owner == me, local + 1, 0).astype(F32).astype(BF16)
        wanted = jnp.dot(wanted, by_ka, preferred_element_type=F32)
        wanted = jnp.where(table_row // QL == table_lane // 32, wanted, 0.0)
        wanted = jnp.sum(wanted, axis=0, keepdims=True)
        local_row = (lax.broadcasted_iota(I32, (MINE, DEVS), 0) + 1).astype(F32)
        send_order[:, c * DEVS:(c + 1) * DEVS] = one_hot(local_row == wanted)
        owner = jnp.dot(owner.astype(F32).astype(BF16), by_own, preferred_element_type=F32)
        owner = jnp.where(table_row == pb * QL + table_lane // 32, owner, 0.0)
        owner = jnp.sum(owner, axis=0, keepdims=True)
        device = lax.broadcasted_iota(I32, (DEVS, MINE), 0).astype(F32)
        place_order[c] = one_hot(device == owner)

    own_in(0)
    own_in(1)
    own_in(2)
    own_in(3)

    from_sides(0)
    from_sides(1)
    from_sides(2)
    from_sides(3)

    for s in range(4):
        chi_copy(s, s).wait_recv()

    def scaled(re, im, cols):
        chi_re, chi_im = chi[0, 0:1, cols], chi[0, 1:2, cols]
        return (re * chi_re - im * chi_im).astype(BF16), (re * chi_im + im * chi_re).astype(BF16)

    for j in range(4):
        at = j * ROWS
        rows = whole[:, rows_of((1 - core) * 16 + j * 4 + x), :]
        base[:, at:at + ROWS, :] = rows
        re, im = scaled(rows[0].astype(F32), rows[1].astype(F32), slice(0, K))
        left_even[at:at + ROWS, :] = re
        left_even[MINE + at:MINE + at + ROWS, :] = im

    for s in range(4):
        for plane in range(2):
            piece = piece_at(s, 2)
            pass_plane(piece, plane, send3.at[s, 6 + plane], partner).wait_recv()
            pass_plane(piece, plane, send3.at[s, 6 + plane], partner).start()
    for i in range(16):
        for plane in range(2):
            pass_plane(core * 16 + i, plane, send3.at[0, 0], partner).wait_recv()
    pl.semaphore_signal(known_half, inc=1, device_id=across, device_id_type=MESH)

    def product(left_op, n):
        cols = slice(n * NB, (n + 1) * NB)
        by_re = jnp.dot(left_op[...], whole[0, :, cols], preferred_element_type=F32)
        by_im = jnp.dot(left_op[...], whole[1, :, cols], preferred_element_type=F32)
        return by_re[:MINE] - by_im[MINE:], by_im[:MINE] + by_re[MINE:]

    def step(now, later):
        for n in range(K // NB):
            cols = slice(n * NB, (n + 1) * NB)
            re, im = product(now, n)
            re, im = scaled(base[0, :, cols].astype(F32) + re, base[1, :, cols].astype(F32) + im, cols)
            later[0:MINE, cols] = re
            later[MINE:2 * MINE, cols] = im

    def two_steps(i, carry):
        step(left_even, left_odd)
        step(left_odd, left_even)

        @pl.when(i == 0)
        def _():
            pl.semaphore_wait(known_half, 1)
            pl.semaphore_signal(known_all, inc=1, device_id=mirror, device_id_type=MESH)

        return carry

    lax.fori_loop(0, LADDER // 2 - 1, two_steps, 0)
    step(left_even, left_odd)

    def home_copy(h, s):
        j = (y + s) % 4
        return pltpu.make_async_remote_copy(
            src_ref=outgoing.at[h, j],
            dst_ref=home.at[h, y],
            send_sem=send_home.at[h, s],
            recv_sem=recv_home.at[h, y],
            device_id=giver(j),
            device_id_type=MESH,
        )

    def from_home(h, j):
        return pltpu.make_async_remote_copy(
            src_ref=outgoing.at[h, j],
            dst_ref=home.at[h, j],
            send_sem=send_home.at[h, j],
            recv_sem=recv_home.at[h, j],
            device_id=taker(j),
            device_id_type=MESH,
        )

    for n in range(K // NB):
        re, im = product(left_odd, n)
        h = n * NB // HALF
        cols = slice(n * NB % HALF, n * NB % HALF + NB)
        for j in range(4):
            outgoing[h, j, 0, :, cols] = re[j * ROWS:(j + 1) * ROWS].astype(BF16)
            outgoing[h, j, 1, :, cols] = im[j * ROWS:(j + 1) * ROWS].astype(BF16)
        if (n + 1) * NB % HALF == 0:
            for s in range(4):
                home_copy(h, s).start()

    for s in range(4):
        chi_copy(s, s).wait_send()
        for plane in range(2):
            copy1(s, plane).wait_send()
        for t in range(6):
            pass_plane(piece_at(s, 0), 0, send2.at[s, t], right).wait_send()
        for t in range(8):
            pass_plane(piece_at(s, 0), 0, send3.at[s, t], partner).wait_send()

    def row_copy(h, target):
        return pltpu.make_async_remote_copy(
            src_ref=packed.at[h, target],
            dst_ref=arrived.at[h, me],
            send_sem=send_row.at[h],
            recv_sem=recv_row.at[h],
            device_id=(target // 32, target % 32),
            device_id_type=MESH,
        )

    def own_copy(h):
        return pltpu.make_async_copy(packed.at[h, me], arrived.at[h, me], own_row.at[h])

    def others(h):
        return pltpu.make_async_remote_copy(
            src_ref=packed.at[h, pl.ds(0, DEVS - 1)],
            dst_ref=arrived.at[h, pl.ds(0, DEVS - 1)],
            send_sem=send_row.at[h],
            recv_sem=recv_row.at[h],
            device_id=right,
            device_id_type=MESH,
        )

    for h in range(2):
        for s in range(4):
            from_home(h, s).wait_recv()
        if h == 0:
            pl.semaphore_wait(known_all, 1)
        for p in range(2):
            rows = home[h, :, p].reshape(MINE, HALF)
            ordered = lax.dot_general(send_order[...], rows, OVER_ROWS, preferred_element_type=F32)
            for c in range(2):
                for b in range(BLOCKS):
                    stage[pl.ds((c * 2 + p) * BLOCKS + b, DEVS, stride=TILE), :] = ordered[
                        c * DEVS:(c + 1) * DEVS, b * LANES:(b + 1) * LANES
                    ]

        def pack(t):
            packed[h, t] = stage[pl.ds(pl.multiple_of(t * TILE, TILE), TILE), :].astype(BF16)

        def send(i, carry):
            target = (me + i) % DEVS
            pack(target)
            row_copy(h, target).start()
            return carry

        lax.fori_loop(1, DEVS, send, 0)
        pack(me)
        own_copy(h).start()

    for copy in loads:
        copy.wait()
    for h in range(2):
        for p in range(2):
            for q in range(QL):
                out_ref[p, q, :, h * HALF:(h + 1) * HALF] += home[h, q, p].astype(F32)

    for h in range(2):
        others(h).wait_recv()
        own_copy(h).wait()

        def unpack(t, carry):
            stage[pl.ds(pl.multiple_of(t * TILE, TILE), TILE), :] = arrived[h, t].astype(F32)
            return carry

        lax.fori_loop(0, DEVS, unpack, 0, unroll=8)
        for b in range(4 * BLOCKS):
            lined_up[:, b * LANES:(b + 1) * LANES] = stage[pl.ds(b, DEVS, stride=TILE), :].astype(BF16)
        for c, sum_ref in enumerate((out_a_ref, out_b_ref)):
            for p in range(2):
                rows = lined_up[:, (c * 2 + p) * HALF:(c * 2 + p + 1) * HALF]
                placed[p * MINE:(p + 1) * MINE, :] = lax.dot_general(
                    place_order[c], rows, OVER_ROWS, preferred_element_type=F32
                ).astype(BF16)
            for n in range(K // NB):
                cols = slice(n * NB, (n + 1) * NB)
                moved = jnp.dot(
                    placed[...], selector[c, h * HALF:(h + 1) * HALF, cols], preferred_element_type=F32
                )
                sum_ref[:, :, :, cols] += moved.reshape(2, QL, ROWS, NB)

    for h in range(2):
        others(h).wait_send()
        for s in range(4):
            home_copy(h, s).wait_send()


def run_ladder(vertex, cross_a, cross_b, bubble, row_maps, col_maps):
    out = jax.ShapeDtypeStruct(vertex.shape, F32)
    hbm, vmem = pl.BlockSpec(memory_space=pltpu.HBM), pl.BlockSpec(memory_space=pltpu.VMEM)
    return pl.pallas_call(
        ladder_kernel,
        out_shape=(out, out, out),
        in_specs=[hbm, vmem, hbm, hbm, vmem, vmem, vmem],
        out_specs=(vmem, vmem, vmem),
        scratch_shapes=[
            pltpu.VMEM((2, K, K), BF16),
            pltpu.VMEM((2, MINE, K), BF16),
            pltpu.VMEM((2 * MINE, K), BF16),
            pltpu.VMEM((2 * MINE, K), BF16),
            pltpu.VMEM((2, QL, 2, ROWS, HALF), BF16),
            pltpu.VMEM((2, QL, 2, ROWS, HALF), BF16),
            pltpu.VMEM((QL, 2, K), F32),
            pltpu.VMEM((QL, 2, K), F32),
            pltpu.VMEM((2, K, K), BF16),
            pltpu.VMEM((MINE, 2 * DEVS), BF16),
            pltpu.VMEM((2, DEVS, MINE), BF16),
            pltpu.VMEM((DEVS * TILE, LANES), F32),
            pltpu.VMEM((2, DEVS, TILE, LANES), BF16),
            pltpu.VMEM((2, DEVS, TILE, LANES), BF16),
            pltpu.VMEM((DEVS, 4 * HALF), BF16),
            pltpu.VMEM((2 * MINE, HALF), BF16),
            pltpu.SemaphoreType.DMA((3,)),
            pltpu.SemaphoreType.DMA((4, 2)),
            pltpu.SemaphoreType.DMA((4,)),
            pltpu.SemaphoreType.DMA((4,)),
            pltpu.SemaphoreType.DMA((2, 32)),
            pltpu.SemaphoreType.DMA((4, 6)),
            pltpu.SemaphoreType.DMA((4, 8)),
            pltpu.SemaphoreType.DMA((2, 4)),
            pltpu.SemaphoreType.DMA((2, 4)),
            pltpu.SemaphoreType.DMA((2,)),
            pltpu.SemaphoreType.DMA((2,)),
            pltpu.SemaphoreType.DMA((2,)),
            pltpu.SemaphoreType.REGULAR,
            pltpu.SemaphoreType.REGULAR,
        ],
        compiler_params=pltpu.CompilerParams(
            collective_id=0, has_side_effects=True, vmem_limit_bytes=50 * 2**20
        ),
    )(vertex, vertex.astype(BF16), cross_a, cross_b, bubble, row_maps, col_maps)


def hand_over_kernel(*refs):
    done = refs[-1]
    copies = [
        pltpu.make_async_copy(refs[i].at[p], refs[3 + i].at[p], done.at[i, p])
        for i in range(3) for p in range(2)
    ]
    for copy in copies:
        copy.start()
    for copy in copies:
        copy.wait()


def per_device(*args):
    results = run_ladder(*args)
    shape = jax.ShapeDtypeStruct(args[0].shape, F32)
    return tuple(pl.pallas_call(
        hand_over_kernel,
        out_shape=(shape,) * 3,
        in_specs=[pl.BlockSpec(memory_space=pltpu.VMEM)] * 3,
        out_specs=(pl.BlockSpec(memory_space=pltpu.HBM),) * 3,
        scratch_shapes=[pltpu.SemaphoreType.DMA((3, 2))],
        compiler_params=pltpu.CompilerParams(vmem_limit_bytes=50 * 2**20),
    )(*results))


def solution(mesh):
    return jax.shard_map(
        per_device,
        mesh=mesh,
        in_specs=(
            P(None, "pb", "ka", None),
            P(None, "pb", "ka", None),
            P(None, "pb", "ka", None),
            P(None, "pb", None),
            P(),
            P(),
        ),
        out_specs=(P(None, "pb", "ka", None), P(None, "pb", "ka", None), P(None, "pb", "ka", None)),
        check_vma=False,
    )
```

```python
import jax
import jax.numpy as jnp
from jax import lax
from jax.experimental import pallas as pl
from jax.experimental.pallas import tpu as pltpu
from jax.sharding import PartitionSpec as P

LADDER = 6
MESH = pl.DeviceIdType.MESH
BF16 = jnp.bfloat16
F32 = jnp.float32
I32 = jnp.int32
K = 1024
ROWS = 32
QL = 4
MINE = QL * ROWS
NB = 256
DEVS = 128
LANES = 128
HALF = K // 2
TILE = 16
BLOCKS = HALF // LANES
OVER_ROWS = (((0,), (0,)), ((), ()))


def one_hot(hit):
    return jnp.where(hit, 1.0, 0.0).astype(BF16)


def ladder_kernel(
    vertex_ref, low, a_ref, b_ref, bubble, rows_from, cols_from, out_ref, out_a_ref, out_b_ref,
    whole, base, left_even, left_odd, outgoing, home, chi_own, chi, selector, send_order, place_order,
    stage, packed, arrived, lined_up, placed,
    load, send1, send_chi, recv_chi, recv, send2, send3, send_home, recv_home,
    send_row, recv_row, own_row, known_half, known_all,
):
    pb, ka = lax.axis_index("pb"), lax.axis_index("ka")
    z_hi, core = pb // 2, pb % 2
    z_lo, y, x = ka // 16, (ka // 4) % 4, ka % 4
    line = ka - x
    me = pb * 32 + ka

    def taker(j):
        return (z_hi * 2 + 1 - z_lo, core * 16 + j * 4 + x)

    def giver(j):
        return (z_hi * 2 + z_lo, (1 - core) * 16 + j * 4 + x)

    right = (pb, line + (x + 1) % 4)
    left = (pb, line + (x + 3) % 4)
    partner = (z_hi * 2 + 1 - core, ka)
    across = (pb, (ka + 16) % 32)
    mirror = ((pb + 2) % 4, ka)

    loads = [
        pltpu.make_async_copy(source, target, load.at[i])
        for i, (source, target) in enumerate(((vertex_ref, out_ref), (a_ref, out_a_ref), (b_ref, out_b_ref)))
    ]
    barrier = pltpu.get_barrier_semaphore()
    for j in range(4):
        pl.semaphore_signal(barrier, inc=1, device_id=taker(j), device_id_type=MESH)
        pl.semaphore_signal(barrier, inc=1, device_id=giver(j), device_id_type=MESH)
    for other in (right, left, partner, across, mirror):
        pl.semaphore_signal(barrier, inc=1, device_id=other, device_id_type=MESH)
    for j in range(QL):
        chi_own[j] = bubble[:, j]
    pl.semaphore_wait(barrier, 13)

    def rows_of(piece):
        return pl.ds(pl.multiple_of(piece * ROWS, ROWS), ROWS)

    def copy1(s, plane):
        j = (y + s) % 4
        return pltpu.make_async_remote_copy(
            src_ref=low.at[plane, j],
            dst_ref=whole.at[plane, rows_of(ka), :],
            send_sem=send1.at[s, plane],
            recv_sem=recv.at[plane, ka],
            device_id=taker(j),
            device_id_type=MESH,
        )

    def chi_copy(s, slot):
        j = (y + s) % 4
        return pltpu.make_async_remote_copy(
            src_ref=chi_own.at[j],
            dst_ref=chi.at[slot],
            send_sem=send_chi.at[s],
            recv_sem=recv_chi.at[slot],
            device_id=taker(j),
            device_id_type=MESH,
        )

    def pass_plane(piece, plane, sem, target):
        block = whole.at[plane, rows_of(piece), :]
        return pltpu.make_async_remote_copy(
            src_ref=block,
            dst_ref=block,
            send_sem=sem,
            recv_sem=recv.at[plane, piece],
            device_id=target,
            device_id_type=MESH,
        )

    def piece_at(s, shift):
        return (1 - core) * 16 + (y + 4 - s) % 4 * 4 + (x + shift) % 4

    for s in range(4):
        for plane in range(2):
            copy1(s, plane).start()
    for s in range(4):
        chi_copy(s, y).start()

    def own_in(s):
        piece = piece_at(s, 0)
        for plane in range(2):
            pass_plane(piece, plane, send2.at[s, plane], right).wait_recv()
            pass_plane(piece, plane, send2.at[s, plane], right).start()
            pass_plane(piece, plane, send2.at[s, 2 + plane], left).start()
            pass_plane(piece, plane, send3.at[s, plane], partner).start()

    def from_sides(s):
        for plane in range(2):
            for side, target in ((3, right), (1, left)):
                piece = piece_at(s, side)
                slot = 2 + side - 1 + plane
                pass_plane(piece, plane, send3.at[s, slot], partner).wait_recv()
                if (plane == 0) == (side == 3):
                    pass_plane(piece, plane, send2.at[s, 4 + plane], target).start()
                pass_plane(piece, plane, send3.at[s, slot], partner).start()

    def select_rows(i, carry):
        at = pl.multiple_of(i * ROWS, ROWS)
        source = lax.broadcasted_iota(I32, (ROWS, K), 0) + at
        for c in range(2):
            selector[c, pl.ds(at, ROWS), :] = one_hot(source == cols_from[c:c + 1, :])
        return carry

    lax.fori_loop(0, K // ROWS, select_rows, 0)
    at_row = lax.broadcasted_iota(I32, (K, LANES), 0)
    at_lane = lax.broadcasted_iota(I32, (K, LANES), 1)
    by_ka = one_hot((at_lane % 32) == (at_row // 32))
    by_own = one_hot(((at_lane % 32) == (at_row % 32)) & ((at_row // 32) == ka))
    table_row = lax.broadcasted_iota(I32, (16, LANES), 0)
    table_lane = lax.broadcasted_iota(I32, (16, LANES), 1)
    for c in range(2):
        table = rows_from[c]
        owner = table // (QL * K) * 32 + table % K // ROWS
        local = table // K % QL * ROWS + table % ROWS
        wanted = jnp.where(owner == me, local + 1, 0).astype(F32).astype(BF16)
        wanted = jnp.dot(wanted, by_ka, preferred_element_type=F32)
        wanted = jnp.where(table_row // QL == table_lane // 32, wanted, 0.0)
        wanted = jnp.sum(wanted, axis=0, keepdims=True)
        local_row = (lax.broadcasted_iota(I32, (MINE, DEVS), 0) + 1).astype(F32)
        send_order[:, c * DEVS:(c + 1) * DEVS] = one_hot(local_row == wanted)
        owner = jnp.dot(owner.astype(F32).astype(BF16), by_own, preferred_element_type=F32)
        owner = jnp.where(table_row == pb * QL + table_lane // 32, owner, 0.0)
        owner = jnp.sum(owner, axis=0, keepdims=True)
        device = lax.broadcasted_iota(I32, (DEVS, MINE), 0).astype(F32)
        place_order[c] = one_hot(device == owner)

    own_in(0)
    own_in(1)
    own_in(2)
    own_in(3)
    for copy in loads:
        copy.start()

    from_sides(0)
    from_sides(1)
    from_sides(2)
    from_sides(3)

    for s in range(4):
        chi_copy(s, s).wait_recv()

    def scaled(re, im, cols):
        chi_re, chi_im = chi[0, 0:1, cols], chi[0, 1:2, cols]
        return (re * chi_re - im * chi_im).astype(BF16), (re * chi_im + im * chi_re).astype(BF16)

    for j in range(4):
        at = j * ROWS
        rows = whole[:, rows_of((1 - core) * 16 + j * 4 + x), :]
        base[:, at:at + ROWS, :] = rows
        re, im = scaled(rows[0].astype(F32), rows[1].astype(F32), slice(0, K))
        left_even[at:at + ROWS, :] = re
        left_even[MINE + at:MINE + at + ROWS, :] = im

    for s in range(4):
        for plane in range(2):
            piece = piece_at(s, 2)
            pass_plane(piece, plane, send3.at[s, 6 + plane], partner).wait_recv()
            pass_plane(piece, plane, send3.at[s, 6 + plane], partner).start()
    for i in range(16):
        for plane in range(2):
            pass_plane(core * 16 + i, plane, send3.at[0, 0], partner).wait_recv()
    pl.semaphore_signal(known_half, inc=1, device_id=across, device_id_type=MESH)

    def product(left_op, n):
        cols = slice(n * NB, (n + 1) * NB)
        by_re = jnp.dot(left_op[...], whole[0, :, cols], preferred_element_type=F32)
        by_im = jnp.dot(left_op[...], whole[1, :, cols], preferred_element_type=F32)
        return by_re[:MINE] - by_im[MINE:], by_im[:MINE] + by_re[MINE:]

    def step(now, later):
        for n in range(K // NB):
            cols = slice(n * NB, (n + 1) * NB)
            re, im = product(now, n)
            re, im = scaled(base[0, :, cols].astype(F32) + re, base[1, :, cols].astype(F32) + im, cols)
            later[0:MINE, cols] = re
            later[MINE:2 * MINE, cols] = im

    def two_steps(i, carry):
        step(left_even, left_odd)
        step(left_odd, left_even)

        @pl.when(i == 0)
        def _():
            pl.semaphore_wait(known_half, 1)
            pl.semaphore_signal(known_all, inc=1, device_id=mirror, device_id_type=MESH)

        return carry

    lax.fori_loop(0, LADDER // 2 - 1, two_steps, 0)
    step(left_even, left_odd)

    def home_copy(h, s):
        j = (y + s) % 4
        return pltpu.make_async_remote_copy(
            src_ref=outgoing.at[h, j],
            dst_ref=home.at[h, y],
            send_sem=send_home.at[h, s],
            recv_sem=recv_home.at[h, y],
            device_id=giver(j),
            device_id_type=MESH,
        )

    def from_home(h, j):
        return pltpu.make_async_remote_copy(
            src_ref=outgoing.at[h, j],
            dst_ref=home.at[h, j],
            send_sem=send_home.at[h, j],
            recv_sem=recv_home.at[h, j],
            device_id=taker(j),
            device_id_type=MESH,
        )

    for n in range(K // NB):
        re, im = product(left_odd, n)
        h = n * NB // HALF
        cols = slice(n * NB % HALF, n * NB % HALF + NB)
        for j in range(4):
            outgoing[h, j, 0, :, cols] = re[j * ROWS:(j + 1) * ROWS].astype(BF16)
            outgoing[h, j, 1, :, cols] = im[j * ROWS:(j + 1) * ROWS].astype(BF16)
        if (n + 1) * NB % HALF == 0:
            for s in range(4):
                home_copy(h, s).start()

    for s in range(4):
        chi_copy(s, s).wait_send()
        for plane in range(2):
            copy1(s, plane).wait_send()
        for t in range(6):
            pass_plane(piece_at(s, 0), 0, send2.at[s, t], right).wait_send()
        for t in range(8):
            pass_plane(piece_at(s, 0), 0, send3.at[s, t], partner).wait_send()

    def row_copy(h, target):
        return pltpu.make_async_remote_copy(
            src_ref=packed.at[h, target],
            dst_ref=arrived.at[h, me],
            send_sem=send_row.at[h],
            recv_sem=recv_row.at[h],
            device_id=(target // 32, target % 32),
            device_id_type=MESH,
        )

    def own_copy(h):
        return pltpu.make_async_copy(packed.at[h, me], arrived.at[h, me], own_row.at[h])

    def others(h):
        return pltpu.make_async_remote_copy(
            src_ref=packed.at[h, pl.ds(0, DEVS - 1)],
            dst_ref=arrived.at[h, pl.ds(0, DEVS - 1)],
            send_sem=send_row.at[h],
            recv_sem=recv_row.at[h],
            device_id=right,
            device_id_type=MESH,
        )

    for h in range(2):
        for s in range(4):
            from_home(h, s).wait_recv()
        if h == 0:
            pl.semaphore_wait(known_all, 1)
        for p in range(2):
            rows = home[h, :, p].reshape(MINE, HALF)
            ordered = lax.dot_general(send_order[...], rows, OVER_ROWS, preferred_element_type=F32)
            for c in range(2):
                for b in range(BLOCKS):
                    stage[pl.ds((c * 2 + p) * BLOCKS + b, DEVS, stride=TILE), :] = ordered[
                        c * DEVS:(c + 1) * DEVS, b * LANES:(b + 1) * LANES
                    ]

        def pack(t):
            packed[h, t] = stage[pl.ds(pl.multiple_of(t * TILE, TILE), TILE), :].astype(BF16)

        def send(i, carry):
            target = (me + i) % DEVS
            pack(target)
            row_copy(h, target).start()
            return carry

        lax.fori_loop(1, DEVS, send, 0)
        pack(me)
        own_copy(h).start()

    for copy in loads:
        copy.wait()
    for h in range(2):
        for p in range(2):
            for q in range(QL):
                out_ref[p, q, :, h * HALF:(h + 1) * HALF] += home[h, q, p].astype(F32)

    for h in range(2):
        others(h).wait_recv()
        own_copy(h).wait()

        def unpack(t, carry):
            stage[pl.ds(pl.multiple_of(t * TILE, TILE), TILE), :] = arrived[h, t].astype(F32)
            return carry

        lax.fori_loop(0, DEVS, unpack, 0, unroll=8)
        for b in range(4 * BLOCKS):
            lined_up[:, b * LANES:(b + 1) * LANES] = stage[pl.ds(b, DEVS, stride=TILE), :].astype(BF16)
        for c, sum_ref in enumerate((out_a_ref, out_b_ref)):
            for p in range(2):
                rows = lined_up[:, (c * 2 + p) * HALF:(c * 2 + p + 1) * HALF]
                placed[p * MINE:(p + 1) * MINE, :] = lax.dot_general(
                    place_order[c], rows, OVER_ROWS, preferred_element_type=F32
                ).astype(BF16)
            for n in range(K // NB):
                cols = slice(n * NB, (n + 1) * NB)
                moved = jnp.dot(
                    placed[...], selector[c, h * HALF:(h + 1) * HALF, cols], preferred_element_type=F32
                )
                sum_ref[:, :, :, cols] += moved.reshape(2, QL, ROWS, NB)

    for h in range(2):
        others(h).wait_send()
        for s in range(4):
            home_copy(h, s).wait_send()


def run_ladder(vertex, cross_a, cross_b, bubble, row_maps, col_maps):
    out = jax.ShapeDtypeStruct(vertex.shape, F32)
    hbm, vmem = pl.BlockSpec(memory_space=pltpu.HBM), pl.BlockSpec(memory_space=pltpu.VMEM)
    return pl.pallas_call(
        ladder_kernel,
        out_shape=(out, out, out),
        in_specs=[hbm, vmem, hbm, hbm, vmem, vmem, vmem],
        out_specs=(vmem, vmem, vmem),
        scratch_shapes=[
            pltpu.VMEM((2, K, K), BF16),
            pltpu.VMEM((2, MINE, K), BF16),
            pltpu.VMEM((2 * MINE, K), BF16),
            pltpu.VMEM((2 * MINE, K), BF16),
            pltpu.VMEM((2, QL, 2, ROWS, HALF), BF16),
            pltpu.VMEM((2, QL, 2, ROWS, HALF), BF16),
            pltpu.VMEM((QL, 2, K), F32),
            pltpu.VMEM((QL, 2, K), F32),
            pltpu.VMEM((2, K, K), BF16),
            pltpu.VMEM((MINE, 2 * DEVS), BF16),
            pltpu.VMEM((2, DEVS, MINE), BF16),
            pltpu.VMEM((DEVS * TILE, LANES), F32),
            pltpu.VMEM((2, DEVS, TILE, LANES), BF16),
            pltpu.VMEM((2, DEVS, TILE, LANES), BF16),
            pltpu.VMEM((DEVS, 4 * HALF), BF16),
            pltpu.VMEM((2 * MINE, HALF), BF16),
            pltpu.SemaphoreType.DMA((3,)),
            pltpu.SemaphoreType.DMA((4, 2)),
            pltpu.SemaphoreType.DMA((4,)),
            pltpu.SemaphoreType.DMA((4,)),
            pltpu.SemaphoreType.DMA((2, 32)),
            pltpu.SemaphoreType.DMA((4, 6)),
            pltpu.SemaphoreType.DMA((4, 8)),
            pltpu.SemaphoreType.DMA((2, 4)),
            pltpu.SemaphoreType.DMA((2, 4)),
            pltpu.SemaphoreType.DMA((2,)),
            pltpu.SemaphoreType.DMA((2,)),
            pltpu.SemaphoreType.DMA((2,)),
            pltpu.SemaphoreType.REGULAR,
            pltpu.SemaphoreType.REGULAR,
        ],
        compiler_params=pltpu.CompilerParams(
            collective_id=0, has_side_effects=True, vmem_limit_bytes=50 * 2**20
        ),
    )(vertex, vertex.astype(BF16), cross_a, cross_b, bubble, row_maps, col_maps)


def hand_over_kernel(*refs):
    done = refs[-1]
    copies = [
        pltpu.make_async_copy(refs[i].at[p], refs[3 + i].at[p], done.at[i, p])
        for i in range(3) for p in range(2)
    ]
    for copy in copies:
        copy.start()
    for copy in copies:
        copy.wait()


def per_device(*args):
    results = run_ladder(*args)
    shape = jax.ShapeDtypeStruct(args[0].shape, F32)
    return tuple(pl.pallas_call(
        hand_over_kernel,
        out_shape=(shape,) * 3,
        in_specs=[pl.BlockSpec(memory_space=pltpu.VMEM)] * 3,
        out_specs=(pl.BlockSpec(memory_space=pltpu.HBM),) * 3,
        scratch_shapes=[pltpu.SemaphoreType.DMA((3, 2))],
        compiler_params=pltpu.CompilerParams(vmem_limit_bytes=50 * 2**20),
    )(*results))


def solution(mesh):
    return jax.shard_map(
        per_device,
        mesh=mesh,
        in_specs=(
            P(None, "pb", "ka", None),
            P(None, "pb", "ka", None),
            P(None, "pb", "ka", None),
            P(None, "pb", None),
            P(),
            P(),
        ),
        out_specs=(P(None, "pb", "ka", None), P(None, "pb", "ka", None), P(None, "pb", "ka", None)),
        check_vma=False,
    )
```
